32 devices in a mesh: doc: 4 (over z), seq: 8 (over y, x, core).
Axes of the slice: x: 2, y: 2, z: 4, core: 2. Of those that a mesh axis runs over, the one named last changes fastest.
Arguments:
- features: bfloat16 [4096, 1280], P(('doc', 'seq')), parts along dimension 0, may hold values from -6 to 6
- gate_in: bfloat16 [4096, 1024], P(('doc', 'seq')), parts along dimension 0, may hold values from -6 to 6
- conv_weight: float32 [4, 1280], replicated, may hold values from -3 to 3
- conv_bias: float32 [1280], replicated, may hold values from -0.5 to 0.5
- log_decay: float32 [4096, 16], P(('doc', 'seq')), parts along dimension 0, may hold values from -0.6 to 0
- step_size: float32 [4096, 16], P(('doc', 'seq')), parts along dimension 0, may hold values from 0 to 2
- gate_gain: float32 [1024], replicated, may hold values from 0.25 to 1.75
- w_out: bfloat16 [1024, 1024], replicated, may hold values from -0.1875 to 0.1875
- boundaries: int32 [1024], P('doc'), parts along dimension 0, may hold values from 0 to 1023, as said below
- pad_vector: bfloat16 [512], replicated, may hold values from -5 to 5
- main_gain: float32 [1536], replicated, may hold values from 0.25 to 1.75
- w_gate: bfloat16 [1536, 4096], P(None, 'seq'), may hold values from -0.15625 to 0.15625
- w_up: bfloat16 [1536, 4096], P(None, 'seq'), may hold values from -0.15625 to 0.15625
- w_down: bfloat16 [4096, 1024], P('seq'), may hold values from -0.09375 to 0.09375
Outputs:
- byte_out: bfloat16 [4096, 1024], P(('doc', 'seq')), parts along dimension 0
The draws below stay inside these ranges and needn't reach their ends.
There are 4 independent parts, one for each index of `doc`. The reference program is written for one: setup_inputs(seed, part) draws one part's arguments, and reference() takes and returns one part's arrays. A program takes and returns all parts, laid end to end along the dimension named above; an argument that names none is the same for every part. Nothing has to cross between parts.
Inputs may be any that keep to these rules, and one draw needn't show every extreme that they name: Strictly increasing, boundaries[0] = 0. For every k = 1, 2, ..., the number of entries below k * 128 lies between k * 32 and k * 32 + 31, and the upper end is reached at some k in every draw. The bytes of one device hold 1 to 63 entries, and some device holds exactly 63.
All inputs are finite; a program needn't handle non-finite values.
Results may differ from the reference program's by a relative error of at most 0.02.
Values may be sent and summed in bfloat16 or wider, within the bound.
A program may use at most 64 MiB of HBM per device.

```python
import math
import jax
import jax.numpy as jnp
from jax import lax

D = 1024
HALF_HEADS = 16
HEAD = 64
STATE = 128
KW = 4
D2 = 1536
FF = 4096
BYTES_DEV = 128
DI = 1024
XBC = 1280
PAD = 512
CH_DEV = 32
BYTES = 1024
N_SEQ = 8


def decay_pair(key):
    base_key = jax.random.fold_in(key, 17)
    key_fast, key_rough, random_key_location, random_key_depth, key_step = jax.random.split(base_key, 5)
    overall_row_count = BYTES_DEV * N_SEQ
    fast_heads = jax.random.bernoulli(key_fast, 0.5, (HALF_HEADS,))
    roughness = jnp.exp(jax.random.uniform(key_rough, (overall_row_count, HALF_HEADS), jnp.float32, math.log(0.6), math.log(1.8)))
    rate_increment = jnp.where(fast_heads[None, :], 1.0 / 40.0, 0.3 / overall_row_count) * roughness
    surge_locations = jax.random.randint(random_key_location, (3,), 0, overall_row_count)
    surge_present = jnp.any(lax.iota(jnp.int32, overall_row_count)[:, None] == surge_locations[None, :], axis=1)
    surge_depth = jax.random.uniform(random_key_depth, (overall_row_count, HALF_HEADS), jnp.float32, 0.22, 0.5)
    logarithm_decays = -rate_increment - jnp.where(surge_present[:, None], surge_depth, 0.0)
    factor = jnp.exp(jax.random.uniform(key_step, (overall_row_count, HALF_HEADS), jnp.float32, math.log(0.5), math.log(2.0)))
    steps_drawn = factor * jnp.sqrt(1.0 - jnp.exp(2.0 * logarithm_decays))
    return (logarithm_decays, steps_drawn)


def draw_log_decay(key, part):
    return decay_pair(key)[0]


def draw_step_size(key, part):
    return decay_pair(key)[1]


def shuffle_one(perm_key):
    return jax.random.permutation(perm_key, BYTES_DEV)


def draw_boundaries(key, part):
    base_key = jax.random.fold_in(key, 29)
    key_offsets, key_peak, key_perm = jax.random.split(base_key, 3)
    offsets = jax.random.randint(key_offsets, (N_SEQ,), 0, CH_DEV)
    peak_dev = jax.random.randint(key_peak, (), 0, N_SEQ - 1)
    dev_ids = lax.iota(jnp.int32, N_SEQ)
    offsets = jnp.where(dev_ids == peak_dev, CH_DEV - 1, offsets)
    offsets = jnp.where(dev_ids == peak_dev - 1, 0, offsets)
    offsets = jnp.where(dev_ids == N_SEQ - 1, 0, offsets)
    prior_offsets = jnp.concatenate([jnp.zeros((1,), jnp.int32), offsets[:-1]])
    counts = CH_DEV + offsets - prior_offsets
    perm_keys = jax.random.split(key_perm, N_SEQ)
    orders = jax.vmap(shuffle_one)(perm_keys)
    byte_ranks = jnp.argsort(orders, axis=1).astype(jnp.int32)
    byte_ranks = byte_ranks.at[0, 0].set(-1)
    byte_ranks = jnp.argsort(jnp.argsort(byte_ranks, axis=1), axis=1).astype(jnp.int32)
    chosen_flags = (byte_ranks < counts[:, None]).reshape(N_SEQ * BYTES_DEV)
    return jnp.nonzero(chosen_flags, size=N_SEQ * CH_DEV)[0].astype(jnp.int32)


def level_of(own_key, shape, cuts, low, top_value):
    def one(axis_at, parts):
        heights = jax.random.uniform(jax.random.fold_in(jax.random.fold_in(own_key, 6), axis_at), (parts,), jnp.float32, low / len(cuts), top_value / len(cuts))
        return jnp.repeat(jnp.exp(heights), shape[axis_at] // parts).reshape((-1,) + (1,) * (len(shape) - axis_at - 1))

    factor_of = one(*cuts[0])
    for cut in cuts[1:]:
        factor_of = factor_of * one(*cut)
    return factor_of


def normal_values(rng, dims, spread, limit, pieces=(), held_as=jnp.bfloat16):
    drawn = jax.random.normal(rng, dims, jnp.float32) * spread
    if len(pieces) > 0:
        drawn = level_of(rng, dims, pieces, -0.22, 0.18) * drawn
    return jnp.clip(drawn, min=-limit, max=limit).astype(held_as)


def setup_inputs(seed: int = 0, part: int = 0) -> dict:
    streams_of = jax.random.split(jax.random.key(seed), 15)
    part_keys = jax.random.split(jax.random.fold_in(streams_of[14], part), 15)
    features = normal_values(part_keys[0], (BYTES, XBC), 1.0, 6.0, ((0, 8),))
    gate_in = normal_values(part_keys[1], (BYTES, DI), 1.0, 6.0, ((0, 8),))
    conv_weight = normal_values(streams_of[2], (KW, XBC), 0.5, 3.0, (), jnp.float32)
    conv_bias = jnp.clip(jax.random.uniform(streams_of[3], (XBC,), jnp.float32, -0.5, 0.5), -0.5, 0.5)
    log_decay = draw_log_decay(jax.random.fold_in(jax.random.fold_in(streams_of[14], part), 71), part)
    step_size = draw_step_size(jax.random.fold_in(jax.random.fold_in(streams_of[14], part), 71), part)
    gate_gain = jnp.clip(1.0 + 0.15 * jax.random.normal(streams_of[6], (DI,), jnp.float32), 0.25, 1.75)
    w_out = normal_values(streams_of[7], (DI, D), DI ** -0.5, 0.1875)
    boundaries = draw_boundaries(jax.random.fold_in(jax.random.fold_in(streams_of[14], part), 71), part)
    pad_vector = normal_values(streams_of[9], (PAD,), 1.0, 5.0)
    main_gain = jnp.clip(1.0 + 0.15 * jax.random.normal(streams_of[10], (D2,), jnp.float32), 0.25, 1.75)
    w_gate = normal_values(streams_of[11], (D2, FF), D2 ** -0.5, 0.15625, ((1, 8),))
    w_up = normal_values(streams_of[12], (D2, FF), D2 ** -0.5, 0.15625, ((1, 8),))
    w_down = normal_values(streams_of[13], (FF, D), FF ** -0.5, 0.09375, ((0, 8),))
    return dict(features=features, gate_in=gate_in, conv_weight=conv_weight, conv_bias=conv_bias, log_decay=log_decay, step_size=step_size, gate_gain=gate_gain, w_out=w_out, boundaries=boundaries, pad_vector=pad_vector, main_gain=main_gain, w_gate=w_gate, w_up=w_up, w_down=w_down)


EPSILON = 1e-05

def rms_scale(values):
    return values * lax.rsqrt(lax.optimization_barrier(jnp.mean(values * values, axis=-1, keepdims=True)) + EPSILON)

def reference(features, gate_in, conv_weight, conv_bias, log_decay, step_size, gate_gain, w_out, boundaries, pad_vector, main_gain, w_gate, w_up, w_down):
    overall_row_count = features.shape[0]
    padded = jnp.concatenate([jnp.zeros((KW - 1, XBC), jnp.bfloat16), features], 0)
    conv_mixed = conv_bias[None, :] + jnp.zeros((overall_row_count, XBC), jnp.float32)
    for tap_index in range(KW):
        conv_mixed = conv_mixed + conv_weight[tap_index][None, :] * padded[tap_index:tap_index + overall_row_count].astype(jnp.float32)
    conv_mixed = jax.nn.silu(conv_mixed).astype(jnp.bfloat16)
    x_part = conv_mixed[:, :DI].astype(jnp.float32).reshape(overall_row_count, HALF_HEADS, HEAD)
    b_part = conv_mixed[:, DI:DI + STATE].astype(jnp.float32)
    c_part = conv_mixed[:, DI + STATE:].astype(jnp.float32)

    def advance(ssm_state, step_inputs):
        decay_now, step_now, x_row, b_row, c_row = step_inputs
        ssm_state = jnp.exp(decay_now)[:, None, None] * ssm_state + (step_now[:, None] * x_row)[:, :, None] * b_row[None, None, :]
        read_out = jnp.einsum('hpn,n->hp', ssm_state, c_row, precision=lax.Precision.HIGHEST)
        return (ssm_state, read_out)
    initial = jnp.zeros((HALF_HEADS, HEAD, STATE), jnp.float32)
    _, ssm_out = lax.scan(advance, initial, (log_decay, step_size, x_part, b_part, c_part))
    gated_out = ssm_out.reshape(overall_row_count, DI) * jax.nn.silu(gate_in.astype(jnp.float32))
    normed = (rms_scale(gated_out) * gate_gain).astype(jnp.bfloat16)
    encoded = jnp.dot(normed, w_out, preferred_element_type=jnp.float32).astype(jnp.bfloat16)
    block_rows = jnp.take(encoded, boundaries.astype(jnp.int32), axis=0)
    filler = jnp.broadcast_to(pad_vector[None, :], (block_rows.shape[0], PAD))
    joined = jnp.concatenate([block_rows, filler], 1)
    main_normed = (rms_scale(joined.astype(jnp.float32)) * main_gain).astype(jnp.bfloat16)
    gate_part = jnp.dot(main_normed, w_gate, preferred_element_type=jnp.float32)
    up_part = jnp.dot(main_normed, w_up, preferred_element_type=jnp.float32)
    activated = (jax.nn.silu(gate_part) * up_part).astype(jnp.bfloat16)
    group_width = FF // N_SEQ
    act_groups = activated.reshape(activated.shape[0], N_SEQ, group_width).transpose(1, 0, 2)
    down_groups = w_down.reshape(N_SEQ, group_width, D)

    def add_group(total, group_inputs):
        act_piece, down_piece = group_inputs
        partial_value = jnp.dot(act_piece, down_piece, preferred_element_type=jnp.float32).astype(jnp.bfloat16)
        return (total + partial_value.astype(jnp.float32), None)
    mlp_out, _ = lax.scan(add_group, jnp.zeros((activated.shape[0], D), jnp.float32), (act_groups, down_groups))
    block_out = (block_rows.astype(jnp.float32) + mlp_out).astype(jnp.bfloat16)
    positions = jnp.arange(overall_row_count).astype(jnp.int32)
    block_of = (jnp.searchsorted(boundaries.astype(jnp.int32), positions, side='right') - 1).astype(jnp.int32)
    expanded = jnp.take(block_out, block_of, axis=0)
    return (encoded.astype(jnp.float32) + expanded.astype(jnp.float32)).astype(jnp.bfloat16)
```

```python
import functools

import jax
import jax.numpy as jnp
from jax import lax
from jax.experimental import pallas as pl
from jax.experimental.pallas import tpu as pltpu
from jax.sharding import PartitionSpec as P

EPSILON = 1e-05
TILE = 16
F32 = jnp.float32
BF16 = jnp.bfloat16


def mm(a, b):
    return jnp.dot(a, b, preferred_element_type=F32)


def silu(v):
    return v / (1.0 + jnp.exp(-v))


def flip(index, mask, count):
    if count & (count - 1):
        return lax.rem(index + mask, count)
    bit, result = 1, index
    while bit < count:
        if mask & bit:
            result = result + (1 - 2 * lax.rem(lax.div(index, bit), 2)) * bit
        bit *= 2
    return result


def unflip(index, mask, count):
    if count & (count - 1):
        return lax.rem(index + count - mask, count)
    return flip(index, mask, count)


def kernel(
    n,
    per,
    features_hbm,
    gate_in_hbm,
    conv_weight_hbm,
    conv_bias_hbm,
    log_decay_hbm,
    step_size_hbm,
    gate_gain_hbm,
    w_out_hbm,
    boundaries_hbm,
    pad_vector_hbm,
    main_gain_hbm,
    w_gate_hbm,
    w_up_hbm,
    w_down_hbm,
    out,
    feat_x,
    feat_bc,
    halo_x,
    halo_bc,
    gate_in,
    conv_weight,
    conv_bias,
    log_decay,
    step_size,
    gate_gain,
    w_out,
    boundaries,
    pad_vector,
    main_gain,
    w_gate,
    w_up,
    w_down,
    xs,
    x_buf,
    bc_buf,
    dec,
    sbuf,
    rbuf,
    obuf,
    inbuf,
    base_out,
    coef_out,
    gated,
    picked,
    own_half,
    enc,
    gath,
    part,
    own_part,
    sums,
    last_part,
    last_sums,
    table,
    load_sem,
    core_send,
    core_recv,
    halo_send,
    halo_recv,
    dec_send,
    dec_recv,
    st1_send,
    st1_recv,
    st2_send,
    st2_recv,
    ag_send,
    ag_recv,
    rs_send,
    rs_recv,
    last_send,
    last_recv,
):
    me = lax.axis_index("seq")
    chips = n // 2
    chip, core = lax.div(me, 2), lax.rem(me, 2)
    other = 1 - core
    partner = chip * 2 + other
    rows, half = feat_x.shape[1:]
    both = 2 * rows
    state_dim = feat_bc.shape[2] // 2
    inner = 2 * half
    channels = half + 2 * state_dim
    heads = log_decay.shape[1]
    head_dim = half // heads
    piece = state_dim // chips
    taps = conv_weight.shape[0]
    window = gath.shape[1]
    width = out.shape[1]

    barrier = pltpu.get_barrier_semaphore()
    for off in range(1, n):
        pl.semaphore_signal(
            barrier,
            inc=1,
            device_id={"seq": lax.rem(me + off, n)},
            device_id_type=pl.DeviceIdType.MESH,
        )

    def columns(which):
        return pl.ds(pl.multiple_of(which * half, half), half)

    def head_rows(which):
        return pl.ds(pl.multiple_of(which * heads, heads), heads)

    loads = {}

    def load(name, src, dst):
        c = pltpu.make_async_copy(src, dst, load_sem.at[len(loads)])
        c.start()
        loads[name] = c

    bc_columns = pl.ds(inner, 2 * state_dim)
    load("decay", log_decay_hbm.at[head_rows(core)], log_decay.at[core])
    load("step", step_size_hbm.at[head_rows(core)], step_size.at[core])
    load("x", features_hbm.at[:, columns(core)], feat_x.at[core])
    load("bc", features_hbm.at[:, bc_columns], feat_bc.at[core])
    load("taps", conv_weight_hbm, conv_weight)
    load("bias", conv_bias_hbm, conv_bias)
    load("bounds", boundaries_hbm, boundaries)
    load("gate_in", gate_in_hbm.at[:, columns(core)], gate_in.at[core])
    load("gate_gain", gate_gain_hbm, gate_gain)
    load("w_out", w_out_hbm, w_out)
    load("pad", pad_vector_hbm, pad_vector)
    load("main_gain", main_gain_hbm, main_gain)
    load("w_gate", w_gate_hbm, w_gate.at[core])
    load("w_up", w_up_hbm, w_up.at[core])
    load("w_down", w_down_hbm, w_down.at[core])

    def remote(src, dst, ssem, rsem, peer):
        return pltpu.make_async_remote_copy(
            src_ref=src,
            dst_ref=dst,
            send_sem=ssem,
            recv_sem=rsem,
            device_id={"seq": peer},
            device_id_type=pl.DeviceIdType.MESH,
        )

    def same_core(which):
        return which * 2 + core

    pl.semaphore_wait(barrier, n - 1)

    exchange = {}

    def swap(name, src, dst):
        i = len(exchange)
        exchange[name] = remote(src, dst, core_send.at[i], core_recv.at[i], partner)
        exchange[name].start()

    halo_rows = pl.ds(rows - TILE, TILE)
    halos = []
    nxt = lax.rem(chip + 1, chips)
    for k in range(2):
        halos.append(
            remote(
                features_hbm.at[halo_rows, pl.ds(k * half, half)],
                halo_x,
                halo_send.at[2 * k],
                halo_recv.at[0],
                2 * nxt + k,
            )
        )
        halos.append(
            remote(
                features_hbm.at[halo_rows, bc_columns],
                halo_bc,
                halo_send.at[2 * k + 1],
                halo_recv.at[1],
                2 * nxt + k,
            )
        )

    @pl.when((core == 1) & (chip < chips - 1))
    def _():
        for c in halos:
            c.start()

    swap("decay", log_decay_hbm.at[head_rows(other)], log_decay.at[core])
    swap("x", features_hbm.at[:, columns(other)], feat_x.at[core])
    swap("bc", features_hbm.at[:, bc_columns], feat_bc.at[core])
    swap("step", step_size_hbm.at[head_rows(other)], step_size.at[core])
    swap("gate_in", gate_in_hbm.at[:, columns(other)], gate_in.at[core])

    @pl.when(chip == 0)
    def _():
        halo_x[...] = jnp.zeros(halo_x.shape, BF16)
        halo_bc[...] = jnp.zeros(halo_bc.shape, BF16)

    row_i = lax.broadcasted_iota(jnp.int32, (rows, rows), 0)
    col_i = lax.broadcasted_iota(jnp.int32, (rows, rows), 1)
    causal = row_i >= col_i
    loads["decay"].wait()
    exchange["decay"].wait_recv()
    cum = jnp.dot(
        log_decay[...].reshape(2 * heads, rows),
        (row_i <= col_i).astype(F32),
        preferred_element_type=F32,
        precision=lax.Precision.HIGHEST,
    )
    cum = [cum[:heads], cum[heads:]]
    total = [c[:, rows - 1 :] for c in cum]
    mid = [c[:, rows // 2 : rows // 2 + 1] for c in cum]
    dec[chip] = jnp.broadcast_to(total[0] + total[1], dec.shape[1:])
    masks = range(1, chips)
    dec_copies = []
    for m in masks:
        q = flip(chip, m, chips)
        c = remote(dec.at[chip], dec.at[chip], dec_send.at[q], dec_recv.at[chip], same_core(q))
        c.start()
        dec_copies.append(c)

    hid = lax.rem(lax.broadcasted_iota(jnp.int32, (2 * heads, half), 0), heads) * head_dim
    lane = lax.broadcasted_iota(jnp.int32, (2 * heads, half), 1)
    onehot = ((lane >= hid) & (lane < hid + head_dim)).astype(F32).astype(BF16)

    def expand(v):
        hi = v.astype(BF16).astype(F32)
        return mm(jnp.concatenate([hi, v - hi], axis=0).T.astype(BF16), onehot)

    lanes = lax.broadcasted_iota(jnp.int32, (heads, rows), 1)

    def expand_each(values):
        packed = jnp.zeros((heads, rows), F32)
        for i, v in enumerate(values):
            packed = jnp.where(lanes == i, v, packed)
        return expand(packed)

    loads["step"].wait()
    exchange["step"].wait_recv()
    in_coef = [expand(step_size[j] * jnp.exp(mid[j] - cum[j])) for j in range(2)]
    ends = expand_each(
        [
            jnp.exp(total[0] - mid[0]),
            jnp.exp(total[1]),
            jnp.exp(total[1] - mid[1]),
            jnp.exp(mid[1]),
        ]
    )

    def my_columns(v):
        v = jnp.concatenate(
            [jnp.where(core == 0, v[:, :half], v[:, half:inner]), v[:, inner:]], axis=1
        )
        return v

    for name in ("taps", "bias", "x", "bc"):
        loads[name].wait()
    for name in ("x", "bc"):
        exchange[name].wait_recv()
    for j in range(2):
        xs[pl.ds(TILE + j * rows, rows), :half] = feat_x[j].astype(F32)
        xs[pl.ds(TILE + j * rows, rows), half:] = feat_bc[j].astype(F32)
    weight = my_columns(conv_weight[...])
    bias = my_columns(conv_bias[...].reshape(1, inner + 2 * state_dim))

    def convolved(first, count):
        mixed = bias
        for k in range(taps):
            mixed = mixed + weight[k : k + 1] * xs[
                pl.ds(TILE - taps + 1 + first + k, count), :
            ]
        mixed = silu(mixed)
        j, at = first // rows, first % rows
        coef = in_coef[j][at : at + count]
        x_new = (mixed[:, :half].astype(BF16).astype(F32) * coef).astype(BF16)
        x_buf[pl.ds(first, count), :] = x_new
        bc_buf[pl.ds(first, count), :] = mixed[:, half:].astype(BF16)
        b_new = mixed[:, half : half + state_dim]
        return mm(b_new.T.astype(BF16), x_new)

    state_b = convolved(rows, rows)
    state_a = convolved(TILE, rows - TILE)

    @pl.when(chip > 0)
    def _():
        for i, dst in enumerate((halo_x, halo_bc)):
            remote(dst, dst, halo_send.at[i], halo_recv.at[i], partner).wait_recv()

    xs[pl.ds(0, TILE), :half] = halo_x[...].astype(F32)
    xs[pl.ds(0, TILE), half:] = halo_bc[...].astype(F32)
    state_a = (state_a + convolved(0, TILE)) * ends[0:1]
    state = state_a * ends[1:2] + state_b * ends[2:3]
    for j in range(chips):
        sbuf[j] = state[j * piece : (j + 1) * piece].astype(BF16)
    st1 = []
    for m in masks:
        q = flip(chip, m, chips)
        st1.append(
            remote(sbuf.at[q], rbuf.at[chip], st1_send.at[q], st1_recv.at[chip], same_core(q))
        )

    @pl.when(chip < chips - 1)
    def _():
        for c in st1:
            c.start()

    swap("w_gate", w_gate_hbm, w_gate.at[core])
    swap("w_up", w_up_hbm, w_up.at[core])
    swap("w_down", w_down_hbm, w_down.at[core])
    rbuf[chip] = sbuf[chip]

    loads["gate_in"].wait()
    exchange["gate_in"].wait_recv()
    state_mid = state_a.astype(BF16)
    for j in range(2):
        at = pl.ds(j * rows, rows)
        b_part = bc_buf[at, :state_dim]
        c_part = bc_buf[at, state_dim:]
        prod = lax.dot_general(
            c_part, b_part, (((1,), (1,)), ((), ())), preferred_element_type=F32
        )
        local = mm(jnp.where(causal, prod, 0.0).astype(BF16), x_buf[at, :])
        if j == 1:
            local = local + mm(c_part, state_mid) * ends[3:4]
        gate = silu(gate_in[j].astype(F32))
        base_out[at, :] = local * expand(jnp.exp(cum[j] - mid[j])) * gate
        start = cum[j] if j == 0 else cum[j] + total[0]
        coef_out[at, :] = expand(jnp.exp(start)) * gate

    loads["bounds"].wait()
    bnd = boundaries[...].reshape(1, boundaries.shape[0])

    def count(flags):
        return jnp.sum(flags.astype(F32), axis=1, keepdims=True).astype(jnp.int32)

    first_block = count(bnd < chip * both)
    end_block = count(bnd < (chip + 1) * both)

    def slots_of(pos):
        slot = count(bnd <= pos) - 1 - first_block
        return slot, jnp.where(slot < window - 1, slot, slot + 1)

    pos = chip * both + lax.broadcasted_iota(jnp.int32, (both, 1), 0)
    starts = count(bnd == pos) > 0
    slot, entry = slots_of(pos)
    is_last = slot == end_block - 1 - first_block
    at = lax.broadcasted_iota(jnp.int32, (both, 2 * window), 1)
    at = jnp.where(at < window, at + core * window, at + (other - 1) * window)
    chosen = (entry == at) | ((at == window - 1) & is_last)
    pick = jnp.where(chosen & starts, 1.0, 0.0).T.astype(BF16)
    slot, entry = slots_of(me * rows + lax.broadcasted_iota(jnp.int32, (rows, 1), 0))
    entry = jnp.where(slot < 0, window - 1, entry)
    spread = jnp.where(
        entry == lax.broadcasted_iota(jnp.int32, (rows, 2 * window), 1), 1.0, 0.0
    ).astype(BF16)

    for k in range(chips):

        @pl.when(chip != k)
        def _(k=k):
            remote(dec.at[k], dec.at[k], dec_send.at[k], dec_recv.at[k], partner).wait_recv()

    decays = jnp.exp(expand_each([dec[k, :, :1] for k in range(chips)])[:chips])
    for k in range(chips - 1):

        @pl.when(chip != k)
        def _(k=k):
            remote(rbuf.at[k], rbuf.at[k], st1_send.at[k], st1_recv.at[k], partner).wait_recv()

    before = jnp.zeros((piece, half), F32)
    for k in range(chips - 1):
        before = before * decays[k : k + 1] + rbuf[k].astype(F32)
        obuf[k + 1] = before.astype(BF16)
    for k in range(1, chips):

        @pl.when(chip != k)
        def _(k=k):
            remote(
                obuf.at[k], inbuf.at[chip], st2_send.at[k], st2_recv.at[chip], same_core(k)
            ).start()

    @pl.when(chip == 0)
    def _():
        inbuf[...] = jnp.zeros(inbuf.shape, BF16)

    @pl.when(chip > 0)
    def _():
        inbuf[chip] = obuf[chip]
        for m in masks:
            q = unflip(chip, m, chips)
            remote(inbuf.at[q], inbuf.at[q], st2_send.at[q], st2_recv.at[q], partner).wait_recv()

    if piece % TILE == 0:
        state_in = inbuf[...].reshape(state_dim, half)
    else:
        state_in = jnp.concatenate([inbuf[k].astype(F32) for k in range(chips)], axis=0).astype(
            BF16
        )
    carried = mm(bc_buf[:, state_dim:], state_in)
    gated[...] = (base_out[...] + carried * coef_out[...]).astype(BF16)
    rows_out = mm(pick, gated[...]).astype(BF16)
    picked[pl.ds(2, 1)] = rows_out[window:].reshape(1, window, half)
    swap("picked", picked.at[2], picked.at[core])
    their_rows = pl.ds(pl.multiple_of(other * rows, rows), rows)
    my_rows = pl.ds(pl.multiple_of(core * rows, rows), rows)
    swap("gated", gated.at[their_rows], own_half.at[core])
    picked[core] = rows_out[:window]
    own_half[core] = gated[my_rows, :]

    def project(pair):
        v = jnp.concatenate([pair[0].astype(F32), pair[1].astype(F32)], axis=1)
        scale = lax.rsqrt(jnp.mean(v * v, axis=1, keepdims=True) + EPSILON)
        gain = gate_gain[...].reshape(1, inner)
        return mm((v * scale * gain).astype(BF16), w_out[...]).astype(BF16)

    loads["gate_gain"].wait()
    loads["w_out"].wait()
    exchange["picked"].wait_recv()
    gath[chip] = project(picked)
    ag = []
    for m in masks:
        q = flip(chip, m, chips)
        c = remote(gath.at[chip], gath.at[chip], ag_send.at[q], ag_recv.at[chip], same_core(q))
        c.start()
        ag.append(c)

    exchange["gated"].wait_recv()
    enc[...] = project(own_half)

    loads["pad"].wait()
    loads["main_gain"].wait()
    main_width = main_gain.shape[0]
    main = main_gain[...].reshape(1, main_width)
    pad = pad_vector[...].astype(F32).reshape(1, main_width - width)
    pad_sum = jnp.sum(pad * pad, axis=1, keepdims=True)
    pad_gain = pad * main[:, width:]

    def feed_forward(rows_in):
        v = rows_in.astype(F32)
        mean = (jnp.sum(v * v, axis=1, keepdims=True) + pad_sum) / main_width
        scale = lax.rsqrt(mean + EPSILON)
        act = jnp.concatenate(
            [(v * scale * main[:, :width]).astype(BF16), (scale * pad_gain).astype(BF16)], axis=1
        )
        total = None
        for k in range(2):
            hidden = silu(mm(act, w_gate[k])) * mm(act, w_up[k])
            down = mm(hidden.astype(BF16), w_down[k])
            total = down if total is None else total + down
        return total

    for name in ("w_gate", "w_up", "w_down"):
        loads[name].wait()
        exchange[name].wait_recv()

    def send_last(source):
        dest = lax.rem(source + 1, chips)
        c = remote(
            last_part.at[source],
            last_sums.at[chip],
            last_send.at[source],
            last_recv.at[chip],
            2 * dest,
        )
        return c, (core == 0) & (source < chips - 1) & (dest != chip)

    def start_last(source):
        c, needed = send_last(source)

        @pl.when(needed)
        def _():
            c.start()

    own = feed_forward(gath[chip])
    own_part[...] = own
    last_part[chip] = own[window - 1 :]
    start_last(chip)
    rs = []
    groups = [[m for m in masks if m < 3], *[[m for m in masks if m - m % 3 == g] for g in range(3, chips, 3)]]
    for group in groups:
        sources = [unflip(chip, m, chips) for m in group]
        for q in sources:
            remote(gath.at[q], gath.at[q], ag_send.at[q], ag_recv.at[q], partner).wait_recv()
        result = feed_forward(jnp.concatenate([gath[q] for q in sources], axis=0))
        for i, q in enumerate(sources):
            piece_out = result[i * window : (i + 1) * window]
            part[q] = piece_out.astype(BF16)
            c = remote(part.at[q], sums.at[chip], rs_send.at[q], rs_recv.at[chip], same_core(q))
            c.start()
            rs.append(c)
            last_part[q] = piece_out[window - 1 :]
            start_last(q)

    prev = lax.rem(chip + chips - 1, chips)
    last = gath[prev].astype(F32)[window - 1 :] + last_part[prev]
    for m in masks:
        q = unflip(chip, m, chips)

        @pl.when((core == 0) & (chip > 0))
        def _(q=q):
            remote(
                last_sums.at[q], last_sums.at[q], last_send.at[q], last_recv.at[q], partner
            ).wait_recv()

        last = last + last_sums[q]
    result = gath[chip].astype(F32) + own_part[...]
    for m in masks:
        q = unflip(chip, m, chips)
        remote(sums.at[q], sums.at[q], rs_send.at[q], rs_recv.at[q], partner).wait_recv()
        result = result + sums[q].astype(F32)
    row = lax.broadcasted_iota(jnp.int32, (window, 1), 0)
    result = jnp.where((row == window - 1) & (core == 0) & (chip > 0), last, result)
    table[core] = result.astype(BF16)
    swap("table", table.at[core], table.at[core])
    exchange["table"].wait_recv()
    expanded = mm(spread, table[...].reshape(2 * window, width))
    out[...] = (enc[...].astype(F32) + expanded).astype(BF16)

    for c in [*exchange.values(), *dec_copies, *ag, *rs]:
        c.wait_send()

    @pl.when((core == 1) & (chip < chips - 1))
    def _():
        for c in halos:
            c.wait_send()

    @pl.when(chip < chips - 1)
    def _():
        for c in st1:
            c.wait_send()

    for k in range(1, chips):

        @pl.when(chip != k)
        def _(k=k):
            remote(
                obuf.at[k], inbuf.at[chip], st2_send.at[k], st2_recv.at[chip], same_core(k)
            ).wait_send()

    for k in range(chips - 1):
        c, needed = send_last(k)

        @pl.when(needed)
        def _(c=c):
            c.wait_send()


def per_device(
    n,
    features,
    gate_in,
    conv_weight,
    conv_bias,
    log_decay,
    step_size,
    gate_gain,
    w_out,
    boundaries,
    pad_vector,
    main_gain,
    w_gate,
    w_up,
    w_down,
):
    rows, channels = features.shape
    inner = gate_in.shape[1]
    heads = log_decay.shape[1] // 2
    width = w_out.shape[1]
    bc = channels - inner
    half = inner // 2
    chips = n // 2
    piece = bc // 2 // chips
    per = boundaries.shape[0] // n
    window = 3 * per // 2
    vmem = pl.BlockSpec(memory_space=pltpu.VMEM)
    hbm = pl.BlockSpec(memory_space=pl.ANY)
    dma = pltpu.SemaphoreType.DMA
    args = (
        features,
        gate_in,
        conv_weight,
        conv_bias,
        log_decay.T,
        step_size.T,
        gate_gain,
        w_out,
        boundaries,
        pad_vector,
        main_gain,
        w_gate,
        w_up,
        w_down,
    )

    def like(a):
        return pltpu.VMEM(a.shape, a.dtype)

    def twice(a):
        return pltpu.VMEM((2, *a.shape), a.dtype)

    states = pltpu.VMEM((chips, piece, half), BF16)
    window_rows = pltpu.VMEM((chips, window, width), BF16)
    return pl.pallas_call(
        functools.partial(kernel, n, per),
        out_shape=pltpu.VMEM((rows, width), BF16),
        in_specs=[hbm] * len(args),
        out_specs=vmem,
        scratch_shapes=[
            pltpu.VMEM((2, rows, half), BF16),
            pltpu.VMEM((2, rows, bc), BF16),
            pltpu.VMEM((TILE, half), BF16),
            pltpu.VMEM((TILE, bc), BF16),
            pltpu.VMEM((2, rows, half), BF16),
            like(conv_weight),
            like(conv_bias),
            pltpu.VMEM((2, heads, rows), F32),
            pltpu.VMEM((2, heads, rows), F32),
            like(gate_gain),
            like(w_out),
            like(boundaries),
            like(pad_vector),
            like(main_gain),
            twice(w_gate),
            twice(w_up),
            twice(w_down),
            pltpu.VMEM((TILE + 2 * rows, half + bc), F32),
            pltpu.VMEM((2 * rows, half), BF16),
            pltpu.VMEM((2 * rows, bc), BF16),
            pltpu.VMEM((chips, heads, 128), F32),
            states,
            states,
            states,
            states,
            pltpu.VMEM((2 * rows, half), F32),
            pltpu.VMEM((2 * rows, half), F32),
            pltpu.VMEM((2 * rows, half), BF16),
            pltpu.VMEM((3, window, half), BF16),
            pltpu.VMEM((2, rows, half), BF16),
            pltpu.VMEM((rows, width), BF16),
            window_rows,
            window_rows,
            pltpu.VMEM((window, width), F32),
            window_rows,
            pltpu.VMEM((chips, 1, width), F32),
            pltpu.VMEM((chips, 1, width), F32),
            pltpu.VMEM((2, window, width), BF16),
            dma((16,)),
            dma((16,)),
            dma((16,)),
            dma((4,)),
            dma((2,)),
            *[dma((chips,)) for _ in range(12)],
        ],
        compiler_params=pltpu.CompilerParams(collective_id=0, has_side_effects=True),
    )(*args)


def solution(mesh):
    in_specs = (
        P(("doc", "seq"), None),
        P(("doc", "seq"), None),
        P(),
        P(),
        P(("doc", "seq"), None),
        P(("doc", "seq"), None),
        P(),
        P(),
        P("doc"),
        P(),
        P(),
        P(None, "seq"),
        P(None, "seq"),
        P("seq", None),
    )
    out_specs = P(("doc", "seq"), None)
    return jax.shard_map(
        functools.partial(per_device, mesh.shape["seq"]),
        mesh=mesh,
        in_specs=in_specs,
        out_specs=out_specs,
        check_vma=False,
    )
```

```python
import functools

import jax
import jax.numpy as jnp
from jax import lax
from jax.experimental import pallas as pl
from jax.experimental.pallas import tpu as pltpu
from jax.sharding import PartitionSpec as P

EPSILON = 1e-05
TILE = 16
FULL = 128
F32 = jnp.float32
BF16 = jnp.bfloat16


def mm(a, b):
    return jnp.dot(a, b, preferred_element_type=F32)


def mm_rows(a, w):
    count = a.shape[0]
    short = -count % FULL
    if short:
        a = jnp.concatenate([a, jnp.zeros((short, a.shape[1]), a.dtype)], axis=0)
    return mm(a, w)


def silu(v):
    return v / (1.0 + jnp.exp(-v))


def flip(index, mask, count):
    if count & (count - 1):
        return lax.rem(index + mask, count)
    bit, result = 1, index
    while bit < count:
        if mask & bit:
            result = result + (1 - 2 * lax.rem(lax.div(index, bit), 2)) * bit
        bit *= 2
    return result


def unflip(index, mask, count):
    if count & (count - 1):
        return lax.rem(index + count - mask, count)
    return flip(index, mask, count)


def kernel(
    n,
    per,
    features_hbm,
    gate_in_hbm,
    conv_weight_hbm,
    conv_bias_hbm,
    log_decay_hbm,
    step_size_hbm,
    gate_gain_hbm,
    w_out_hbm,
    boundaries_hbm,
    pad_vector_hbm,
    main_gain_hbm,
    w_gate_hbm,
    w_up_hbm,
    w_down_hbm,
    out,
    feat_x,
    feat_bc,
    halo_x,
    halo_bc,
    gate_in,
    conv_weight,
    conv_bias,
    log_decay,
    step_size,
    gate_gain,
    w_out,
    boundaries,
    pad_vector,
    main_gain,
    w_gate,
    w_up,
    w_down,
    xs,
    x_buf,
    bc_buf,
    dec,
    sbuf,
    rbuf,
    obuf,
    inbuf,
    base_out,
    coef_out,
    gated,
    block_base,
    block_coef,
    block_c,
    picked,
    own_half,
    enc,
    gath,
    own_rows,
    part,
    own_part,
    sums,
    last_part,
    last_sums,
    last_row,
    table,
    load_sem,
    core_send,
    core_recv,
    halo_send,
    halo_recv,
    dec_send,
    dec_recv,
    st1_send,
    st1_recv,
    st2_send,
    st2_recv,
    ag_send,
    ag_recv,
    rs_send,
    rs_recv,
    last_send,
    last_recv,
    ready,
):
    me = lax.axis_index("seq")
    chips = n // 2
    chip, core = lax.div(me, 2), lax.rem(me, 2)
    other = 1 - core
    partner = chip * 2 + other
    rows, half = feat_x.shape[1:]
    both = 2 * rows
    state_dim = feat_bc.shape[2] // 2
    inner = 2 * half
    channels = half + 2 * state_dim
    heads = log_decay.shape[1]
    head_dim = half // heads
    piece = state_dim // chips
    taps = conv_weight.shape[0]
    window = gath.shape[2]
    width = out.shape[1]

    barrier = pltpu.get_barrier_semaphore()
    end = chips - 1

    def tell(semaphore, who):
        pl.semaphore_signal(
            semaphore, inc=1, device_id={"seq": who}, device_id_type=pl.DeviceIdType.MESH
        )

    tell(barrier, partner)

    @pl.when(chip < end)
    def _():
        for q in range(chips):
            for k in range(2):

                @pl.when(chip != q)
                def _(q=q, k=k):
                    tell(barrier, 2 * q + k)

    def columns(which):
        return pl.ds(pl.multiple_of(which * half, half), half)

    def head_rows(which):
        return pl.ds(pl.multiple_of(which * heads, heads), heads)

    loads = {}

    def load(name, src, dst):
        c = pltpu.make_async_copy(src, dst, load_sem.at[len(loads)])
        c.start()
        loads[name] = c

    bc_columns = pl.ds(inner, 2 * state_dim)
    load("decay", log_decay_hbm.at[head_rows(core)], log_decay.at[core])
    load("step", step_size_hbm.at[head_rows(core)], step_size.at[core])
    load("x", features_hbm.at[:, columns(core)], feat_x.at[core])
    load("bc", features_hbm.at[:, bc_columns], feat_bc.at[core])
    load("taps", conv_weight_hbm, conv_weight)
    load("bias", conv_bias_hbm, conv_bias)
    load("bounds", boundaries_hbm, boundaries)
    load("gate_in", gate_in_hbm.at[:, columns(core)], gate_in.at[core])
    load("gate_gain", gate_gain_hbm, gate_gain)
    load("w_out", w_out_hbm, w_out)
    load("pad", pad_vector_hbm, pad_vector)
    load("main_gain", main_gain_hbm, main_gain)
    load("w_gate", w_gate_hbm, w_gate.at[core])
    load("w_up", w_up_hbm, w_up.at[core])
    load("w_down", w_down_hbm, w_down.at[core])

    def remote(src, dst, ssem, rsem, peer):
        return pltpu.make_async_remote_copy(
            src_ref=src,
            dst_ref=dst,
            send_sem=ssem,
            recv_sem=rsem,
            device_id={"seq": peer},
            device_id_type=pl.DeviceIdType.MESH,
        )

    def same_core(which):
        return which * 2 + core

    row_i = lax.broadcasted_iota(jnp.int32, (rows, rows), 0)
    col_i = lax.broadcasted_iota(jnp.int32, (rows, rows), 1)
    causal = row_i >= col_i
    upto = (row_i <= col_i).astype(F32)
    hid = lax.rem(lax.broadcasted_iota(jnp.int32, (2 * heads, half), 0), heads) * head_dim
    lane = lax.broadcasted_iota(jnp.int32, (2 * heads, half), 1)
    onehot = ((lane >= hid) & (lane < hid + head_dim)).astype(F32).astype(BF16)
    lanes = lax.broadcasted_iota(jnp.int32, (heads, rows), 1)

    def expand(v):
        hi = v.astype(BF16).astype(F32)
        return mm(jnp.concatenate([hi, v - hi], axis=0).T.astype(BF16), onehot)

    def expand_each(values):
        packed = jnp.zeros((heads, rows), F32)
        for i, v in enumerate(values):
            packed = jnp.where(lanes == i, v, packed)
        return expand(packed)

    def summed(which):
        return jnp.dot(
            log_decay[which],
            upto,
            preferred_element_type=F32,
            precision=lax.Precision.HIGHEST,
        )

    def in_coefs(which, cum):
        mid = cum[:, rows // 2 : rows // 2 + 1]
        return expand(step_size[which] * jnp.exp(mid - cum))

    loads["decay"].wait()
    own_cum = summed(core)
    loads["step"].wait()
    own_coef = in_coefs(core, own_cum)

    @pl.when(chip < end)
    def _():
        pl.semaphore_wait(barrier, n - 3)

    @pl.when(chip == end)
    def _():
        pl.semaphore_wait(barrier, n - 1)
        for q in range(2 * end):
            tell(ready, q)

    exchange = {}

    def swap(name, src, dst):
        i = len(exchange)
        exchange[name] = remote(src, dst, core_send.at[i], core_recv.at[i], partner)
        exchange[name].start()

    halo_rows = pl.ds(rows - TILE, TILE)
    halos = []
    nxt = lax.rem(chip + 1, chips)
    for k in range(2):
        halos.append(
            remote(
                features_hbm.at[halo_rows, pl.ds(k * half, half)],
                halo_x,
                halo_send.at[2 * k],
                halo_recv.at[0],
                2 * nxt + k,
            )
        )
        halos.append(
            remote(
                features_hbm.at[halo_rows, bc_columns],
                halo_bc,
                halo_send.at[2 * k + 1],
                halo_recv.at[1],
                2 * nxt + k,
            )
        )

    @pl.when((core == 1) & (chip < end - 1))
    def _():
        for c in halos:
            c.start()

    swap("decay", log_decay_hbm.at[head_rows(other)], log_decay.at[core])
    swap("x", features_hbm.at[:, columns(other)], feat_x.at[core])
    swap("bc", features_hbm.at[:, bc_columns], feat_bc.at[core])
    swap("step", step_size_hbm.at[head_rows(other)], step_size.at[core])
    swap("gate_in", gate_in_hbm.at[:, columns(other)], gate_in.at[core])

    @pl.when(chip == 0)
    def _():
        halo_x[...] = jnp.zeros(halo_x.shape, BF16)
        halo_bc[...] = jnp.zeros(halo_bc.shape, BF16)

    def my_columns(v):
        mine = jnp.where(core == 0, v[:, :half], v[:, half:inner])
        return jnp.concatenate([mine, v[:, inner:]], axis=1)

    loads["taps"].wait()
    loads["bias"].wait()
    weight = my_columns(conv_weight[...])
    bias = my_columns(conv_bias[...].reshape(1, inner + 2 * state_dim))

    def convolved(which, first, count, coef):
        mixed = bias
        for k in range(taps):
            mixed = mixed + weight[k : k + 1] * xs[
                which, pl.ds(TILE - taps + 1 + first + k, count), :
            ]
        mixed = silu(mixed)
        x_new = (mixed[:, :half].astype(BF16).astype(F32) * coef).astype(BF16)
        x_buf[which, pl.ds(first, count), :] = x_new
        bc_buf[which, pl.ds(first, count), :] = mixed[:, half:].astype(BF16)
        b_new = mixed[:, half : half + state_dim]
        return mm(b_new.T.astype(BF16), x_new)

    def without_head(which, coef):
        xs[which, pl.ds(TILE, rows), :half] = feat_x[which].astype(F32)
        xs[which, pl.ds(TILE, rows), half:] = feat_bc[which].astype(F32)
        return convolved(which, TILE, rows - TILE, coef[TILE:])

    loads["x"].wait()
    loads["bc"].wait()
    own_state = without_head(core, own_coef)
    exchange["decay"].wait_recv()
    exchange["step"].wait_recv()
    their_cum = summed(other)
    their_coef = in_coefs(other, their_cum)

    def ordered(own, their):
        return jnp.where(core == 0, own, their), jnp.where(core == 0, their, own)

    cum = ordered(own_cum, their_cum)
    total = [c[:, rows - 1 :] for c in cum]
    mid = [c[:, rows // 2 : rows // 2 + 1] for c in cum]
    dec[chip] = jnp.broadcast_to(total[0] + total[1], dec.shape[1:])
    masks = range(1, chips)
    dec_copies = []
    for m in masks:
        q = flip(chip, m, chips)
        dec_copies.append(
            remote(dec.at[chip], dec.at[chip], dec_send.at[q], dec_recv.at[chip], same_core(q))
        )

    @pl.when(chip < end)
    def _():
        pl.semaphore_wait(ready, 2)
        for c in dec_copies:
            c.start()

    @pl.when((core == 1) & (chip == end - 1))
    def _():
        for c in halos:
            c.start()

    ends = expand_each(
        [
            jnp.exp(total[0] - mid[0]),
            jnp.exp(total[0] - mid[0] + total[1]),
            jnp.exp(total[1] - mid[1]),
            jnp.exp(mid[1]),
        ]
    )

    exchange["x"].wait_recv()
    exchange["bc"].wait_recv()
    their_state = without_head(other, their_coef)
    head_coef = ordered(own_coef[:TILE], their_coef[:TILE])
    states = ordered(own_state, their_state)
    xs[1, pl.ds(0, TILE), :half] = feat_x[0, rows - TILE :, :].astype(F32)
    xs[1, pl.ds(0, TILE), half:] = feat_bc[0, rows - TILE :, :].astype(F32)
    late = (states[1] + convolved(1, 0, TILE, head_coef[1])) * ends[2:3]

    @pl.when(chip > 0)
    def _():
        for i, dst in enumerate((halo_x, halo_bc)):
            remote(dst, dst, halo_send.at[i], halo_recv.at[i], partner).wait_recv()

    xs[0, pl.ds(0, TILE), :half] = halo_x[...].astype(F32)
    xs[0, pl.ds(0, TILE), half:] = halo_bc[...].astype(F32)
    state_a = states[0] + convolved(0, 0, TILE, head_coef[0])
    state = state_a * ends[1:2] + late
    for j in range(chips):
        sbuf[j] = state[j * piece : (j + 1) * piece].astype(BF16)
    st1 = []
    for m in masks:
        q = flip(chip, m, chips)
        st1.append(
            remote(sbuf.at[q], rbuf.at[chip], st1_send.at[q], st1_recv.at[chip], same_core(q))
        )

    @pl.when(chip < chips - 1)
    def _():
        for c in st1:
            c.start()

    swap("w_gate", w_gate_hbm, w_gate.at[core])
    swap("w_up", w_up_hbm, w_up.at[core])
    swap("w_down", w_down_hbm, w_down.at[core])
    rbuf[chip] = sbuf[chip]

    loads["bounds"].wait()
    bnd = boundaries[...].reshape(1, boundaries.shape[0])

    def count(flags):
        return jnp.sum(flags.astype(F32), axis=1, keepdims=True).astype(jnp.int32)

    first_block = count(bnd < chip * both)
    end_block = count(bnd < (chip + 1) * both)

    def slots_of(pos):
        slot = count(bnd <= pos) - 1 - first_block
        return slot, jnp.where(slot < window - 1, slot, slot + 1)

    pos = chip * both + lax.broadcasted_iota(jnp.int32, (both, 1), 0)
    starts = count(bnd == pos) > 0
    slot, entry = slots_of(pos)
    is_last = slot == end_block - 1 - first_block
    at = lax.broadcasted_iota(jnp.int32, (both, 2 * window), 1)
    at = jnp.where(at < window, at + core * window, at + (other - 1) * window)
    chosen = (entry == at) | ((at == window - 1) & is_last)
    pick = jnp.where(chosen & starts, 1.0, 0.0).T.astype(BF16)

    for k in range(end):

        @pl.when(chip != k)
        def _(k=k):
            remote(dec.at[k], dec.at[k], dec_send.at[k], dec_recv.at[k], partner).wait_recv()

    decays = jnp.exp(expand_each([dec[k, :, :1] for k in range(end)])[:chips])
    for k in range(chips - 1):

        @pl.when(chip != k)
        def _(k=k):
            remote(rbuf.at[k], rbuf.at[k], st1_send.at[k], st1_recv.at[k], partner).wait_recv()

    before = jnp.zeros((piece, half), F32)
    for k in range(chips - 1):
        before = before * decays[k : k + 1] + rbuf[k].astype(F32)
        obuf[k + 1] = before.astype(BF16)
    for k in range(1, chips):

        @pl.when(chip != k)
        def _(k=k):
            remote(
                obuf.at[k], inbuf.at[chip], st2_send.at[k], st2_recv.at[chip], same_core(k)
            ).start()

    loads["gate_in"].wait()
    exchange["gate_in"].wait_recv()
    state_mid = (state_a * ends[0:1]).astype(BF16)
    for j in range(2):
        at = pl.ds(j * rows, rows)
        b_part = bc_buf[j, :, :state_dim]
        c_part = bc_buf[j, :, state_dim:]
        prod = lax.dot_general(
            c_part, b_part, (((1,), (1,)), ((), ())), preferred_element_type=F32
        )
        local = mm(jnp.where(causal, prod, 0.0).astype(BF16), x_buf[j])
        if j == 1:
            local = local + mm(c_part, state_mid) * ends[3:4]
        gate = silu(gate_in[j].astype(F32))
        base_out[at, :] = local * expand(jnp.exp(cum[j] - mid[j])) * gate
        start = cum[j] if j == 0 else cum[j] + total[0]
        coef_out[at, :] = expand(jnp.exp(start)) * gate

    def pick_exact(v):
        hi = v.astype(BF16)
        return mm(pick, hi) + mm(pick, (v - hi.astype(F32)).astype(BF16))

    block_base[...] = pick_exact(base_out[...])
    block_coef[...] = pick_exact(coef_out[...])
    c_all = bc_buf[:, :, state_dim:].reshape(both, state_dim)
    block_c[...] = mm(pick, c_all).astype(BF16)
    slot, entry = slots_of(me * rows + lax.broadcasted_iota(jnp.int32, (rows, 1), 0))
    entry = jnp.where(slot < 0, window - 1, entry)
    spread = jnp.where(
        entry == lax.broadcasted_iota(jnp.int32, (rows, 2 * window), 1), 1.0, 0.0
    ).astype(BF16)

    @pl.when(chip == 0)
    def _():
        inbuf[...] = jnp.zeros(inbuf.shape, BF16)

    @pl.when(chip > 0)
    def _():
        inbuf[chip] = obuf[chip]
        for m in masks:
            q = unflip(chip, m, chips)
            remote(inbuf.at[q], inbuf.at[q], st2_send.at[q], st2_recv.at[q], partner).wait_recv()

    if piece % TILE == 0:
        state_in = inbuf[...].reshape(state_dim, half)
    else:
        state_in = jnp.concatenate([inbuf[k].astype(F32) for k in range(chips)], axis=0).astype(
            BF16
        )
    carried = mm(block_c[...], state_in)
    rows_out = (block_base[...] + carried * block_coef[...]).astype(BF16)
    gath[chip, core] = rows_out[:window]
    picked[...] = rows_out[window:]
    ag = []
    sends = [m for m in (3, 1, 2) if m < chips] + list(range(4, chips))
    for m in sends:
        q = flip(chip, m, chips)
        for i, (src, to) in enumerate(
            ((gath.at[chip, core], same_core(q)), (picked, 2 * q + other))
        ):
            c = remote(src, gath.at[chip, core], ag_send.at[2 * q + i], ag_recv.at[me], to)
            c.start()
            ag.append(c)
    swap("picked", picked, gath.at[chip, core])

    loads["gate_gain"].wait()
    loads["w_out"].wait()

    def project(pairs):
        v = jnp.concatenate(
            [
                jnp.concatenate([p[0].astype(F32), p[1].astype(F32)], axis=1)
                for p in pairs
            ],
            axis=0,
        )
        scale = lax.rsqrt(jnp.mean(v * v, axis=1, keepdims=True) + EPSILON)
        gain = gate_gain[...].reshape(1, inner)
        normed = (v * scale * gain).astype(BF16)
        return mm_rows(normed, w_out[...])[: v.shape[0]].astype(BF16)


    loads["pad"].wait()
    loads["main_gain"].wait()
    main_width = main_gain.shape[0]
    main = main_gain[...].reshape(1, main_width)
    pad = pad_vector[...].astype(F32).reshape(1, main_width - width)
    pad_sum = jnp.sum(pad * pad, axis=1, keepdims=True)
    pad_gain = pad * main[:, width:]

    def feed_forward(rows_in):
        v = rows_in.astype(F32)
        mean = (jnp.sum(v * v, axis=1, keepdims=True) + pad_sum) / main_width
        scale = lax.rsqrt(mean + EPSILON)
        act = jnp.concatenate(
            [(v * scale * main[:, :width]).astype(BF16), (scale * pad_gain).astype(BF16)], axis=1
        )
        total = None
        for k in range(2):
            hidden = silu(mm_rows(act, w_gate[k])) * mm_rows(act, w_up[k])
            down = mm(hidden.astype(BF16), w_down[k])
            total = down if total is None else total + down
        return total[: v.shape[0]]

    for name in ("w_gate", "w_up", "w_down"):
        loads[name].wait()
        exchange[name].wait_recv()

    def send_last(source):
        dest = lax.rem(source + 1, chips)
        c = remote(
            last_part.at[source],
            last_sums.at[chip],
            last_send.at[source],
            last_recv.at[chip],
            2 * dest,
        )
        return c, (core == 0) & (source < chips - 1) & (dest != chip)

    def start_last(source):
        c, needed = send_last(source)

        @pl.when(needed)
        def _():
            c.start()

    rs = []
    groups = [sends[:1], sends[1:3], *[sends[i : i + 3] for i in range(3, len(sends), 3)]]
    for group in groups:
        sources = [unflip(chip, m, chips) for m in group]
        for q in sources:
            for k in range(2):
                ref = gath.at[q, k]
                remote(ref, ref, ag_send.at[2 * q + k], ag_recv.at[2 * q + k], partner).wait_recv()
        blocks = project([gath.at[q] for q in sources])
        result = feed_forward(blocks)
        for i, q in enumerate(sources):
            piece_out = result[i * window : (i + 1) * window]
            part[q] = piece_out.astype(BF16)
            c = remote(part.at[q], sums.at[chip], rs_send.at[q], rs_recv.at[chip], same_core(q))
            c.start()
            rs.append(c)
            last_part[q] = piece_out[window - 1 :]
            last_row[q] = blocks[(i + 1) * window - TILE : (i + 1) * window].astype(F32)[TILE - 1 :]
            start_last(q)

    gated[...] = (base_out[...] + mm(c_all, state_in) * coef_out[...]).astype(BF16)
    their_rows = pl.ds(pl.multiple_of(other * rows, rows), rows)
    my_rows = pl.ds(pl.multiple_of(core * rows, rows), rows)
    swap("gated", gated.at[their_rows], own_half.at[core])
    own_half[core] = gated[my_rows, :]
    exchange["picked"].wait_recv()
    own_rows[...] = project([gath.at[chip]])
    own = feed_forward(own_rows[...])
    own_part[...] = own
    last_part[chip] = own[window - 1 :]
    start_last(chip)
    exchange["gated"].wait_recv()
    enc[...] = project([own_half])
    prev = lax.rem(chip + chips - 1, chips)
    last = last_row[prev] + last_part[prev]
    for m in masks:
        q = unflip(chip, m, chips)

        @pl.when((core == 0) & (chip > 0))
        def _(q=q):
            remote(
                last_sums.at[q], last_sums.at[q], last_send.at[q], last_recv.at[q], partner
            ).wait_recv()

        last = last + last_sums[q]
    result = own_rows[...].astype(F32) + own_part[...]
    for m in masks:
        q = unflip(chip, m, chips)
        remote(sums.at[q], sums.at[q], rs_send.at[q], rs_recv.at[q], partner).wait_recv()
        result = result + sums[q].astype(F32)
    row = lax.broadcasted_iota(jnp.int32, (window, 1), 0)
    result = jnp.where((row == window - 1) & (core == 0) & (chip > 0), last, result)
    table[core] = result.astype(BF16)
    swap("table", table.at[core], table.at[core])
    exchange["table"].wait_recv()
    expanded = mm(spread, table[...].reshape(2 * window, width))
    out[...] = (enc[...].astype(F32) + expanded).astype(BF16)

    for c in [*exchange.values(), *ag, *rs]:
        c.wait_send()

    @pl.when((core == 1) & (chip < chips - 1))
    def _():
        for c in halos:
            c.wait_send()

    @pl.when(chip < chips - 1)
    def _():
        for c in [*dec_copies, *st1]:
            c.wait_send()

    for k in range(1, chips):

        @pl.when(chip != k)
        def _(k=k):
            remote(
                obuf.at[k], inbuf.at[chip], st2_send.at[k], st2_recv.at[chip], same_core(k)
            ).wait_send()

    for k in range(chips - 1):
        c, needed = send_last(k)

        @pl.when(needed)
        def _(c=c):
            c.wait_send()


def per_device(
    n,
    features,
    gate_in,
    conv_weight,
    conv_bias,
    log_decay,
    step_size,
    gate_gain,
    w_out,
    boundaries,
    pad_vector,
    main_gain,
    w_gate,
    w_up,
    w_down,
):
    rows, channels = features.shape
    inner = gate_in.shape[1]
    heads = log_decay.shape[1] // 2
    width = w_out.shape[1]
    bc = channels - inner
    half = inner // 2
    chips = n // 2
    piece = bc // 2 // chips
    per = boundaries.shape[0] // n
    window = 3 * per // 2
    vmem = pl.BlockSpec(memory_space=pltpu.VMEM)
    hbm = pl.BlockSpec(memory_space=pl.ANY)
    dma = pltpu.SemaphoreType.DMA
    args = (
        features,
        gate_in,
        conv_weight,
        conv_bias,
        log_decay.T,
        step_size.T,
        gate_gain,
        w_out,
        boundaries,
        pad_vector,
        main_gain,
        w_gate,
        w_up,
        w_down,
    )

    def like(a):
        return pltpu.VMEM(a.shape, a.dtype)

    def twice(a):
        return pltpu.VMEM((2, *a.shape), a.dtype)

    states = pltpu.VMEM((chips, piece, half), BF16)
    window_rows = pltpu.VMEM((chips, window, width), BF16)
    return pl.pallas_call(
        functools.partial(kernel, n, per),
        out_shape=pltpu.VMEM((rows, width), BF16),
        in_specs=[hbm] * len(args),
        out_specs=vmem,
        scratch_shapes=[
            pltpu.VMEM((2, rows, half), BF16),
            pltpu.VMEM((2, rows, bc), BF16),
            pltpu.VMEM((TILE, half), BF16),
            pltpu.VMEM((TILE, bc), BF16),
            pltpu.VMEM((2, rows, half), BF16),
            like(conv_weight),
            like(conv_bias),
            pltpu.VMEM((2, heads, rows), F32),
            pltpu.VMEM((2, heads, rows), F32),
            like(gate_gain),
            like(w_out),
            like(boundaries),
            like(pad_vector),
            like(main_gain),
            twice(w_gate),
            twice(w_up),
            twice(w_down),
            pltpu.VMEM((2, TILE + rows, half + bc), F32),
            pltpu.VMEM((2, rows, half), BF16),
            pltpu.VMEM((2, rows, bc), BF16),
            pltpu.VMEM((chips, heads, 128), F32),
            states,
            states,
            states,
            states,
            pltpu.VMEM((2 * rows, half), F32),
            pltpu.VMEM((2 * rows, half), F32),
            pltpu.VMEM((2 * rows, half), BF16),
            pltpu.VMEM((2 * window, half), F32),
            pltpu.VMEM((2 * window, half), F32),
            pltpu.VMEM((2 * window, bc // 2), BF16),
            pltpu.VMEM((window, half), BF16),
            pltpu.VMEM((2, rows, half), BF16),
            pltpu.VMEM((rows, width), BF16),
            pltpu.VMEM((chips, 2, window, half), BF16),
            pltpu.VMEM((window, width), BF16),
            window_rows,
            pltpu.VMEM((window, width), F32),
            window_rows,
            pltpu.VMEM((chips, 1, width), F32),
            pltpu.VMEM((chips, 1, width), F32),
            pltpu.VMEM((chips, 1, width), F32),
            pltpu.VMEM((2, window, width), BF16),
            dma((16,)),
            dma((16,)),
            dma((16,)),
            dma((4,)),
            dma((2,)),
            *[dma((chips,)) for _ in range(6)],
            dma((n,)),
            dma((n,)),
            *[dma((chips,)) for _ in range(4)],
            pltpu.SemaphoreType.REGULAR,
        ],
        compiler_params=pltpu.CompilerParams(collective_id=0, has_side_effects=True),
    )(*args)


def solution(mesh):
    in_specs = (
        P(("doc", "seq"), None),
        P(("doc", "seq"), None),
        P(),
        P(),
        P(("doc", "seq"), None),
        P(("doc", "seq"), None),
        P(),
        P(),
        P("doc"),
        P(),
        P(),
        P(None, "seq"),
        P(None, "seq"),
        P("seq", None),
    )
    out_specs = P(("doc", "seq"), None)
    return jax.shard_map(
        functools.partial(per_device, mesh.shape["seq"]),
        mesh=mesh,
        in_specs=in_specs,
        out_specs=out_specs,
        check_vma=False,
    )
```

```python
import functools

import jax
import jax.numpy as jnp
from jax import lax
from jax.experimental import pallas as pl
from jax.experimental.pallas import tpu as pltpu
from jax.sharding import PartitionSpec as P

EPSILON = 1e-05
TILE = 16
FULL = 128
SPLIT = 2
F32 = jnp.float32
BF16 = jnp.bfloat16


def mm(a, b):
    return jnp.dot(a, b, preferred_element_type=F32)


def mm_rows(a, w):
    count = a.shape[0]
    short = -count % FULL
    if short:
        a = jnp.concatenate([a, jnp.zeros((short, a.shape[1]), a.dtype)], axis=0)
    return mm(a, w)


def silu(v):
    return v / (1.0 + jnp.exp(-v))


def flip(index, mask, count):
    if count & (count - 1):
        return lax.rem(index + mask, count)
    bit, result = 1, index
    while bit < count:
        if mask & bit:
            result = result + (1 - 2 * lax.rem(lax.div(index, bit), 2)) * bit
        bit *= 2
    return result


def unflip(index, mask, count):
    if count & (count - 1):
        return lax.rem(index + count - mask, count)
    return flip(index, mask, count)


def kernel(
    n,
    per,
    features_hbm,
    gate_in_hbm,
    conv_weight_hbm,
    conv_bias_hbm,
    log_decay_hbm,
    step_size_hbm,
    gate_gain_hbm,
    w_out_hbm,
    boundaries_hbm,
    pad_vector_hbm,
    main_gain_hbm,
    w_gate_hbm,
    w_up_hbm,
    w_down_hbm,
    out,
    feat_x,
    feat_bc,
    halo_x,
    halo_bc,
    gate_in,
    conv_weight,
    conv_bias,
    log_decay,
    step_size,
    gate_gain,
    w_out,
    boundaries,
    pad_vector,
    main_gain,
    w_gate,
    w_up,
    w_down,
    xs,
    x_buf,
    bc_buf,
    dec,
    sbuf,
    rbuf,
    obuf,
    inbuf,
    base_out,
    coef_out,
    gated,
    block_base,
    block_coef,
    block_c,
    picked,
    own_half,
    enc,
    gath,
    own_rows,
    part,
    own_part,
    sums,
    last_part,
    last_sums,
    last_row,
    table,
    load_sem,
    core_send,
    core_recv,
    halo_send,
    halo_recv,
    dec_send,
    dec_recv,
    st1_send,
    st1_recv,
    st2_send,
    st2_recv,
    ag_send,
    ag_recv,
    rs_send,
    rs_recv,
    last_send,
    last_recv,
    ready,
):
    me = lax.axis_index("seq")
    chips = n // 2
    chip, core = lax.div(me, 2), lax.rem(me, 2)
    other = 1 - core
    partner = chip * 2 + other
    rows, half = feat_x.shape[1:]
    both = 2 * rows
    state_dim = feat_bc.shape[2] // 2
    inner = 2 * half
    channels = half + 2 * state_dim
    heads = log_decay.shape[1]
    head_dim = half // heads
    piece = state_dim // chips
    taps = conv_weight.shape[0]
    window = gath.shape[2]
    width = out.shape[1]

    barrier = pltpu.get_barrier_semaphore()
    end = chips - 1

    def tell(semaphore, who):
        pl.semaphore_signal(
            semaphore, inc=1, device_id={"seq": who}, device_id_type=pl.DeviceIdType.MESH
        )

    tell(barrier, partner)

    @pl.when(chip < end)
    def _():
        for q in range(chips):
            for k in range(2):

                @pl.when(chip != q)
                def _(q=q, k=k):
                    tell(barrier, 2 * q + k)

    def columns(which):
        return pl.ds(pl.multiple_of(which * half, half), half)

    def head_rows(which):
        return pl.ds(pl.multiple_of(which * heads, heads), heads)

    loads = {}

    def load(name, src, dst):
        c = pltpu.make_async_copy(src, dst, load_sem.at[len(loads)])
        c.start()
        loads[name] = c

    bc_columns = pl.ds(inner, 2 * state_dim)
    load("decay", log_decay_hbm.at[head_rows(core)], log_decay.at[core])
    load("step", step_size_hbm.at[head_rows(core)], step_size.at[core])
    load("x", features_hbm.at[:, columns(core)], feat_x.at[core])
    load("bc", features_hbm.at[:, bc_columns], feat_bc.at[core])
    load("taps", conv_weight_hbm, conv_weight)
    load("bias", conv_bias_hbm, conv_bias)
    load("bounds", boundaries_hbm, boundaries)
    load("gate_in", gate_in_hbm.at[:, columns(core)], gate_in.at[core])
    load("gate_gain", gate_gain_hbm, gate_gain)
    load("w_out", w_out_hbm, w_out)
    load("pad", pad_vector_hbm, pad_vector)
    load("main_gain", main_gain_hbm, main_gain)
    load("w_gate", w_gate_hbm, w_gate.at[core])
    load("w_up", w_up_hbm, w_up.at[core])
    load("w_down", w_down_hbm, w_down.at[core])

    def remote(src, dst, ssem, rsem, peer):
        return pltpu.make_async_remote_copy(
            src_ref=src,
            dst_ref=dst,
            send_sem=ssem,
            recv_sem=rsem,
            device_id={"seq": peer},
            device_id_type=pl.DeviceIdType.MESH,
        )

    def same_core(which):
        return which * 2 + core

    row_i = lax.broadcasted_iota(jnp.int32, (rows, rows), 0)
    col_i = lax.broadcasted_iota(jnp.int32, (rows, rows), 1)
    causal = row_i >= col_i
    upto = (row_i <= col_i).astype(F32).astype(BF16)
    hid = lax.rem(lax.broadcasted_iota(jnp.int32, (2 * heads, half), 0), heads) * head_dim
    lane = lax.broadcasted_iota(jnp.int32, (2 * heads, half), 1)
    onehot = ((lane >= hid) & (lane < hid + head_dim)).astype(F32).astype(BF16)
    lanes = lax.broadcasted_iota(jnp.int32, (heads, rows), 1)

    def expand(v):
        hi = v.astype(BF16).astype(F32)
        return mm(jnp.concatenate([hi, v - hi], axis=0).T.astype(BF16), onehot)

    def expand_each(values):
        packed = jnp.zeros((heads, rows), F32)
        for i, v in enumerate(values):
            packed = jnp.where(lanes == i, v, packed)
        return expand(packed)

    def summed(which):
        v = log_decay[which]
        parts = []
        for _ in range(3):
            parts.append(v.astype(BF16).astype(F32))
            v = v - parts[-1]
        sums = mm(jnp.concatenate(parts, axis=0).astype(BF16), upto)
        return sums[:heads] + sums[heads : 2 * heads] + sums[2 * heads :]

    def in_coefs(which, cum):
        mid = cum[:, rows // 2 : rows // 2 + 1]
        return expand(step_size[which] * jnp.exp(mid - cum))

    loads["decay"].wait()
    own_cum = summed(core)
    loads["step"].wait()
    own_coef = in_coefs(core, own_cum)

    @pl.when(chip < end)
    def _():
        pl.semaphore_wait(barrier, n - 3)

    @pl.when(chip == end)
    def _():
        pl.semaphore_wait(barrier, n - 1)
        for q in range(2 * end):
            tell(ready, q)

    exchange = {}

    def swap(name, src, dst):
        i = len(exchange)
        exchange[name] = remote(src, dst, core_send.at[i], core_recv.at[i], partner)
        exchange[name].start()

    halo_rows = pl.ds(rows - TILE, TILE)
    halos = []
    nxt = lax.rem(chip + 1, chips)
    for k in range(2):
        halos.append(
            remote(
                features_hbm.at[halo_rows, pl.ds(k * half, half)],
                halo_x,
                halo_send.at[2 * k],
                halo_recv.at[0],
                2 * nxt + k,
            )
        )
        halos.append(
            remote(
                features_hbm.at[halo_rows, bc_columns],
                halo_bc,
                halo_send.at[2 * k + 1],
                halo_recv.at[1],
                2 * nxt + k,
            )
        )

    @pl.when((core == 1) & (chip < end - 1))
    def _():
        for c in halos:
            c.start()

    swap("decay", log_decay_hbm.at[head_rows(other)], log_decay.at[core])
    swap("x", features_hbm.at[:, columns(other)], feat_x.at[core])
    swap("bc", features_hbm.at[:, bc_columns], feat_bc.at[core])
    swap("step", step_size_hbm.at[head_rows(other)], step_size.at[core])
    swap("gate_in", gate_in_hbm.at[:, columns(other)], gate_in.at[core])

    @pl.when(chip == 0)
    def _():
        halo_x[...] = jnp.zeros(halo_x.shape, BF16)
        halo_bc[...] = jnp.zeros(halo_bc.shape, BF16)

    def my_columns(v):
        mine = jnp.where(core == 0, v[:, :half], v[:, half:inner])
        return jnp.concatenate([mine, v[:, inner:]], axis=1)

    loads["taps"].wait()
    loads["bias"].wait()
    weight = my_columns(conv_weight[...])
    bias = my_columns(conv_bias[...].reshape(1, inner + 2 * state_dim))

    def convolved(which, first, count, coef):
        mixed = bias
        for k in range(taps):
            mixed = mixed + weight[k : k + 1] * xs[
                which, pl.ds(TILE - taps + 1 + first + k, count), :
            ]
        mixed = silu(mixed)
        x_new = (mixed[:, :half].astype(BF16).astype(F32) * coef).astype(BF16)
        x_buf[which, pl.ds(first, count), :] = x_new
        bc_buf[which, pl.ds(first, count), :] = mixed[:, half:].astype(BF16)
        b_new = mixed[:, half : half + state_dim]
        return mm(b_new.T.astype(BF16), x_new)

    def without_head(which, coef):
        xs[which, pl.ds(TILE, rows), :half] = feat_x[which].astype(F32)
        xs[which, pl.ds(TILE, rows), half:] = feat_bc[which].astype(F32)
        return convolved(which, TILE, rows - TILE, coef[TILE:])

    loads["x"].wait()
    loads["bc"].wait()
    own_state = without_head(core, own_coef)
    exchange["decay"].wait_recv()
    exchange["step"].wait_recv()
    their_cum = summed(other)
    their_coef = in_coefs(other, their_cum)

    def ordered(own, their):
        return jnp.where(core == 0, own, their), jnp.where(core == 0, their, own)

    cum = ordered(own_cum, their_cum)
    total = [c[:, rows - 1 :] for c in cum]
    mid = [c[:, rows // 2 : rows // 2 + 1] for c in cum]
    dec[chip] = jnp.broadcast_to(total[0] + total[1], dec.shape[1:])
    masks = range(1, chips)
    dec_copies = []
    for m in masks:
        q = flip(chip, m, chips)
        dec_copies.append(
            remote(dec.at[chip], dec.at[chip], dec_send.at[q], dec_recv.at[chip], same_core(q))
        )

    @pl.when(chip < end)
    def _():
        pl.semaphore_wait(ready, 2)
        for c in dec_copies:
            c.start()

    @pl.when((core == 1) & (chip == end - 1))
    def _():
        for c in halos:
            c.start()

    ends = expand_each(
        [
            jnp.exp(total[0] - mid[0]),
            jnp.exp(total[0] - mid[0] + total[1]),
            jnp.exp(total[1] - mid[1]),
            jnp.exp(mid[1]),
        ]
    )

    exchange["x"].wait_recv()
    exchange["bc"].wait_recv()
    their_state = without_head(other, their_coef)
    head_coef = ordered(own_coef[:TILE], their_coef[:TILE])
    states = ordered(own_state, their_state)
    xs[1, pl.ds(0, TILE), :half] = feat_x[0, rows - TILE :, :].astype(F32)
    xs[1, pl.ds(0, TILE), half:] = feat_bc[0, rows - TILE :, :].astype(F32)
    late = (states[1] + convolved(1, 0, TILE, head_coef[1])) * ends[2:3]

    @pl.when(chip > 0)
    def _():
        for i, dst in enumerate((halo_x, halo_bc)):
            remote(dst, dst, halo_send.at[i], halo_recv.at[i], partner).wait_recv()

    xs[0, pl.ds(0, TILE), :half] = halo_x[...].astype(F32)
    xs[0, pl.ds(0, TILE), half:] = halo_bc[...].astype(F32)
    state_a = states[0] + convolved(0, 0, TILE, head_coef[0])
    state = state_a * ends[1:2] + late
    part_lanes = half // SPLIT
    for j in range(chips):
        for h in range(SPLIT):
            sbuf[h * chips + j] = state[
                j * piece : (j + 1) * piece, h * part_lanes : (h + 1) * part_lanes
            ].astype(BF16)
    st1 = []
    for h in range(SPLIT):
        for m in masks:
            q = flip(chip, m, chips)
            at, to = h * chips + chip, h * chips + q
            st1.append(
                remote(sbuf.at[to], rbuf.at[at], st1_send.at[to], st1_recv.at[at], same_core(q))
            )

    @pl.when(chip < chips - 1)
    def _():
        for c in st1:
            c.start()

    swap("w_gate", w_gate_hbm, w_gate.at[core])
    swap("w_up", w_up_hbm, w_up.at[core])
    swap("w_down", w_down_hbm, w_down.at[core])
    for h in range(SPLIT):
        rbuf[h * chips + chip] = sbuf[h * chips + chip]

    loads["bounds"].wait()
    bnd = boundaries[...].reshape(1, boundaries.shape[0])

    def count(flags):
        return jnp.sum(flags.astype(F32), axis=1, keepdims=True).astype(jnp.int32)

    first_block = count(bnd < chip * both)
    end_block = count(bnd < (chip + 1) * both)

    def slots_of(pos):
        slot = count(bnd <= pos) - 1 - first_block
        return slot, jnp.where(slot < window - 1, slot, slot + 1)

    pos = chip * both + lax.broadcasted_iota(jnp.int32, (both, 1), 0)
    starts = count(bnd == pos) > 0
    slot, entry = slots_of(pos)
    is_last = slot == end_block - 1 - first_block
    at = lax.broadcasted_iota(jnp.int32, (both, 2 * window), 1)
    at = jnp.where(at < window, at + core * window, at + (other - 1) * window)
    chosen = (entry == at) | ((at == window - 1) & is_last)
    pick = jnp.where(chosen & starts, 1.0, 0.0).T.astype(BF16)

    for k in range(end):

        @pl.when(chip != k)
        def _(k=k):
            remote(dec.at[k], dec.at[k], dec_send.at[k], dec_recv.at[k], partner).wait_recv()

    decays = jnp.exp(expand_each([dec[k, :, :1] for k in range(end)])[:chips])

    def carry(h, k):
        at, to = h * chips + chip, h * chips + k
        return remote(obuf.at[to], inbuf.at[at], st2_send.at[to], st2_recv.at[at], same_core(k))

    for h in range(SPLIT):
        for k in range(end):

            @pl.when(chip != k)
            def _(at=h * chips + k):
                remote(
                    rbuf.at[at], rbuf.at[at], st1_send.at[at], st1_recv.at[at], partner
                ).wait_recv()

        before = jnp.zeros((piece, part_lanes), F32)
        for k in range(end):
            decay = decays[k : k + 1, h * part_lanes : (h + 1) * part_lanes]
            before = before * decay + rbuf[h * chips + k].astype(F32)
            obuf[h * chips + k + 1] = before.astype(BF16)
        for k in range(1, chips):

            @pl.when(chip != k)
            def _(h=h, k=k):
                carry(h, k).start()

    loads["gate_in"].wait()
    exchange["gate_in"].wait_recv()
    state_mid = (state_a * ends[0:1]).astype(BF16)
    for j in range(2):
        at = pl.ds(j * rows, rows)
        b_part = bc_buf[j, :, :state_dim]
        c_part = bc_buf[j, :, state_dim:]
        prod = lax.dot_general(
            c_part, b_part, (((1,), (1,)), ((), ())), preferred_element_type=F32
        )
        local = mm(jnp.where(causal, prod, 0.0).astype(BF16), x_buf[j])
        if j == 1:
            local = local + mm(c_part, state_mid) * ends[3:4]
        gate = silu(gate_in[j].astype(F32))
        base_out[at, :] = local * expand(jnp.exp(cum[j] - mid[j])) * gate
        start = cum[j] if j == 0 else cum[j] + total[0]
        coef_out[at, :] = expand(jnp.exp(start)) * gate

    def pick_exact(v):
        hi = v.astype(BF16)
        return mm(pick, hi) + mm(pick, (v - hi.astype(F32)).astype(BF16))

    block_base[...] = pick_exact(base_out[...])
    block_coef[...] = pick_exact(coef_out[...])
    c_all = bc_buf[:, :, state_dim:].reshape(both, state_dim)
    block_c[...] = mm(pick, c_all).astype(BF16)
    slot, entry = slots_of(me * rows + lax.broadcasted_iota(jnp.int32, (rows, 1), 0))
    entry = jnp.where(slot < 0, window - 1, entry)
    spread = jnp.where(
        entry == lax.broadcasted_iota(jnp.int32, (rows, 2 * window), 1), 1.0, 0.0
    ).astype(BF16)

    @pl.when(chip == 0)
    def _():
        inbuf[...] = jnp.zeros(inbuf.shape, BF16)

    states_in = []
    for h in range(SPLIT):

        @pl.when(chip > 0)
        def _(h=h):
            inbuf[h * chips + chip] = obuf[h * chips + chip]
            for m in masks:
                at = h * chips + unflip(chip, m, chips)
                remote(
                    inbuf.at[at], inbuf.at[at], st2_send.at[at], st2_recv.at[at], partner
                ).wait_recv()

        parts = inbuf[h * chips : (h + 1) * chips]
        if piece % TILE == 0:
            states_in.append(parts.reshape(state_dim, part_lanes))
        else:
            parts = [parts[k].astype(F32) for k in range(chips)]
            states_in.append(jnp.concatenate(parts, axis=0).astype(BF16))

    def carried_by(c):
        return jnp.concatenate([mm(c, state) for state in states_in], axis=1)

    carried = carried_by(block_c[...])
    rows_out = (block_base[...] + carried * block_coef[...]).astype(BF16)
    gath[chip, core] = rows_out[:window]
    picked[...] = rows_out[window:]
    ag = []
    sends = [m for m in (3, 1, 2) if m < chips] + list(range(4, chips))
    for m in sends:
        q = flip(chip, m, chips)
        for i, (src, to) in enumerate(
            ((gath.at[chip, core], same_core(q)), (picked, 2 * q + other))
        ):
            c = remote(src, gath.at[chip, core], ag_send.at[2 * q + i], ag_recv.at[me], to)
            c.start()
            ag.append(c)
    swap("picked", picked, gath.at[chip, core])

    loads["gate_gain"].wait()
    loads["w_out"].wait()

    def project(pairs):
        v = jnp.concatenate(
            [
                jnp.concatenate([p[0].astype(F32), p[1].astype(F32)], axis=1)
                for p in pairs
            ],
            axis=0,
        )
        scale = lax.rsqrt(jnp.mean(v * v, axis=1, keepdims=True) + EPSILON)
        gain = gate_gain[...].reshape(1, inner)
        normed = (v * scale * gain).astype(BF16)
        return mm_rows(normed, w_out[...])[: v.shape[0]].astype(BF16)


    loads["pad"].wait()
    loads["main_gain"].wait()
    main_width = main_gain.shape[0]
    main = main_gain[...].reshape(1, main_width)
    pad = pad_vector[...].astype(F32).reshape(1, main_width - width)
    pad_sum = jnp.sum(pad * pad, axis=1, keepdims=True)
    pad_gain = pad * main[:, width:]

    def hidden_of(rows_in):
        v = rows_in.astype(F32)
        mean = (jnp.sum(v * v, axis=1, keepdims=True) + pad_sum) / main_width
        scale = lax.rsqrt(mean + EPSILON)
        act = jnp.concatenate(
            [(v * scale * main[:, :width]).astype(BF16), (scale * pad_gain).astype(BF16)], axis=1
        )
        return [
            (silu(mm_rows(act, w_gate[k])) * mm_rows(act, w_up[k])).astype(BF16) for k in range(2)
        ]

    span = width // 2

    def part_of(c):
        return slice(c * span, (c + 1) * span)

    def down(hidden, c):
        return mm(hidden[0], w_down[0, :, part_of(c)]) + mm(hidden[1], w_down[1, :, part_of(c)])

    def row_of(parts, at):
        return jnp.concatenate([p[at : at + 1] for p in parts], axis=1)

    for name in ("w_gate", "w_up", "w_down"):
        loads[name].wait()
        exchange[name].wait_recv()

    def send_last(source):
        dest = lax.rem(source + 1, chips)
        c = remote(
            last_part.at[source],
            last_sums.at[chip],
            last_send.at[source],
            last_recv.at[chip],
            2 * dest,
        )
        return c, (core == 0) & (source < chips - 1) & (dest != chip)

    def start_last(source):
        c, needed = send_last(source)

        @pl.when(needed)
        def _():
            c.start()

    rs = []
    groups = [sends[:1], sends[1:3], *[sends[i : i + 3] for i in range(3, len(sends), 3)]]
    for group in groups:
        sources = [unflip(chip, m, chips) for m in group]
        for q in sources:
            for k in range(2):
                ref = gath.at[q, k]
                remote(ref, ref, ag_send.at[2 * q + k], ag_recv.at[2 * q + k], partner).wait_recv()
        blocks = project([gath.at[q] for q in sources])
        hidden = hidden_of(blocks)
        downs = []
        for c in range(2):
            downs.append(down(hidden, c))
            for i, q in enumerate(sources):
                part[c, q] = downs[c][i * window : (i + 1) * window].astype(BF16)
                at, to = c * chips + chip, c * chips + q
                copy = remote(
                    part.at[c, q], sums.at[c, chip], rs_send.at[to], rs_recv.at[at], same_core(q)
                )
                copy.start()
                rs.append(copy)
        for i, q in enumerate(sources):
            last_part[q] = row_of(downs, (i + 1) * window - 1)
            last_row[q] = blocks[(i + 1) * window - TILE : (i + 1) * window].astype(F32)[TILE - 1 :]
            start_last(q)

    gated[...] = (base_out[...] + carried_by(c_all) * coef_out[...]).astype(BF16)
    their_rows = pl.ds(pl.multiple_of(other * rows, rows), rows)
    my_rows = pl.ds(pl.multiple_of(core * rows, rows), rows)
    swap("gated", gated.at[their_rows], own_half.at[core])
    own_half[core] = gated[my_rows, :]
    exchange["picked"].wait_recv()
    own_rows[...] = project([gath.at[chip]])
    hidden = hidden_of(own_rows[...])
    downs = [down(hidden, c) for c in range(2)]
    for c in range(2):
        own_part[c] = downs[c][:window]
    last_part[chip] = row_of(downs, window - 1)
    start_last(chip)
    exchange["gated"].wait_recv()
    enc[...] = project([own_half])
    prev = lax.rem(chip + chips - 1, chips)
    last = last_row[prev] + last_part[prev]
    for m in masks:
        q = unflip(chip, m, chips)

        @pl.when((core == 0) & (chip > 0))
        def _(q=q):
            remote(
                last_sums.at[q], last_sums.at[q], last_send.at[q], last_recv.at[q], partner
            ).wait_recv()

        last = last + last_sums[q]
    row = lax.broadcasted_iota(jnp.int32, (window, 1), 0)
    from_before = (row == window - 1) & (core == 0) & (chip > 0)
    for c in range(2):
        result = own_rows[:, part_of(c)].astype(F32) + own_part[c]
        for m in masks:
            q = unflip(chip, m, chips)
            at, ref = c * chips + q, sums.at[c, q]
            remote(ref, ref, rs_send.at[at], rs_recv.at[at], partner).wait_recv()
            result = result + sums[c, q].astype(F32)
        table[c, core] = jnp.where(from_before, last[:, part_of(c)], result).astype(BF16)
        swap(f"table {c}", table.at[c, core], table.at[c, core])
    for c in range(2):
        exchange[f"table {c}"].wait_recv()
        expanded = mm(spread, table[c].reshape(2 * window, span))
        out[:, part_of(c)] = (enc[:, part_of(c)].astype(F32) + expanded).astype(BF16)

    for c in [*exchange.values(), *ag, *rs]:
        c.wait_send()

    @pl.when((core == 1) & (chip < chips - 1))
    def _():
        for c in halos:
            c.wait_send()

    @pl.when(chip < chips - 1)
    def _():
        for c in [*dec_copies, *st1]:
            c.wait_send()

    for h in range(SPLIT):
        for k in range(1, chips):

            @pl.when(chip != k)
            def _(h=h, k=k):
                carry(h, k).wait_send()

    for k in range(chips - 1):
        c, needed = send_last(k)

        @pl.when(needed)
        def _(c=c):
            c.wait_send()


def per_device(
    n,
    features,
    gate_in,
    conv_weight,
    conv_bias,
    log_decay,
    step_size,
    gate_gain,
    w_out,
    boundaries,
    pad_vector,
    main_gain,
    w_gate,
    w_up,
    w_down,
):
    rows, channels = features.shape
    inner = gate_in.shape[1]
    heads = log_decay.shape[1] // 2
    width = w_out.shape[1]
    bc = channels - inner
    half = inner // 2
    chips = n // 2
    piece = bc // 2 // chips
    per = boundaries.shape[0] // n
    window = 3 * per // 2
    vmem = pl.BlockSpec(memory_space=pltpu.VMEM)
    hbm = pl.BlockSpec(memory_space=pl.ANY)
    dma = pltpu.SemaphoreType.DMA
    args = (
        features,
        gate_in,
        conv_weight,
        conv_bias,
        log_decay.T,
        step_size.T,
        gate_gain,
        w_out,
        boundaries,
        pad_vector,
        main_gain,
        w_gate,
        w_up,
        w_down,
    )

    def like(a):
        return pltpu.VMEM(a.shape, a.dtype)

    def twice(a):
        return pltpu.VMEM((2, *a.shape), a.dtype)

    states = pltpu.VMEM((SPLIT * chips, piece, half // SPLIT), BF16)
    return pl.pallas_call(
        functools.partial(kernel, n, per),
        out_shape=pltpu.VMEM((rows, width), BF16),
        in_specs=[hbm] * len(args),
        out_specs=vmem,
        scratch_shapes=[
            pltpu.VMEM((2, rows, half), BF16),
            pltpu.VMEM((2, rows, bc), BF16),
            pltpu.VMEM((TILE, half), BF16),
            pltpu.VMEM((TILE, bc), BF16),
            pltpu.VMEM((2, rows, half), BF16),
            like(conv_weight),
            like(conv_bias),
            pltpu.VMEM((2, heads, rows), F32),
            pltpu.VMEM((2, heads, rows), F32),
            like(gate_gain),
            like(w_out),
            like(boundaries),
            like(pad_vector),
            like(main_gain),
            twice(w_gate),
            twice(w_up),
            twice(w_down),
            pltpu.VMEM((2, TILE + rows, half + bc), F32),
            pltpu.VMEM((2, rows, half), BF16),
            pltpu.VMEM((2, rows, bc), BF16),
            pltpu.VMEM((chips, heads, 128), F32),
            states,
            states,
            states,
            states,
            pltpu.VMEM((2 * rows, half), F32),
            pltpu.VMEM((2 * rows, half), F32),
            pltpu.VMEM((2 * rows, half), BF16),
            pltpu.VMEM((2 * window, half), F32),
            pltpu.VMEM((2 * window, half), F32),
            pltpu.VMEM((2 * window, bc // 2), BF16),
            pltpu.VMEM((window, half), BF16),
            pltpu.VMEM((2, rows, half), BF16),
            pltpu.VMEM((rows, width), BF16),
            pltpu.VMEM((chips, 2, window, half), BF16),
            pltpu.VMEM((window, width), BF16),
            pltpu.VMEM((2, chips, window, width // 2), BF16),
            pltpu.VMEM((2, window, width // 2), F32),
            pltpu.VMEM((2, chips, window, width // 2), BF16),
            pltpu.VMEM((chips, 1, width), F32),
            pltpu.VMEM((chips, 1, width), F32),
            pltpu.VMEM((chips, 1, width), F32),
            pltpu.VMEM((2, 2, window, width // 2), BF16),
            dma((16,)),
            dma((16,)),
            dma((16,)),
            dma((4,)),
            dma((2,)),
            dma((chips,)),
            dma((chips,)),
            *[dma((SPLIT * chips,)) for _ in range(4)],
            dma((n,)),
            dma((n,)),
            dma((n,)),
            dma((n,)),
            dma((chips,)),
            dma((chips,)),
            pltpu.SemaphoreType.REGULAR,
        ],
        compiler_params=pltpu.CompilerParams(collective_id=0, has_side_effects=True),
    )(*args)


def solution(mesh):
    in_specs = (
        P(("doc", "seq"), None),
        P(("doc", "seq"), None),
        P(),
        P(),
        P(("doc", "seq"), None),
        P(("doc", "seq"), None),
        P(),
        P(),
        P("doc"),
        P(),
        P(),
        P(None, "seq"),
        P(None, "seq"),
        P("seq", None),
    )
    out_specs = P(("doc", "seq"), None)
    return jax.shard_map(
        functools.partial(per_device, mesh.shape["seq"]),
        mesh=mesh,
        in_specs=in_specs,
        out_specs=out_specs,
        check_vma=False,
    )
```

```python
import functools

import jax
import jax.numpy as jnp
from jax import lax
from jax.experimental import pallas as pl
from jax.experimental.pallas import tpu as pltpu
from jax.sharding import PartitionSpec as P

EPSILON = 1e-05
TILE = 16
FULL = 128
SPLIT = 2
F32 = jnp.float32
BF16 = jnp.bfloat16


def mm(a, b):
    return jnp.dot(a, b, preferred_element_type=F32)


def mm_rows(a, w):
    count = a.shape[0]
    short = -count % FULL
    if short:
        a = jnp.concatenate([a, jnp.zeros((short, a.shape[1]), a.dtype)], axis=0)
    return mm(a, w)


def silu(v):
    return v / (1.0 + jnp.exp(-v))


def flip(index, mask, count):
    if count & (count - 1):
        return lax.rem(index + mask, count)
    bit, result = 1, index
    while bit < count:
        if mask & bit:
            result = result + (1 - 2 * lax.rem(lax.div(index, bit), 2)) * bit
        bit *= 2
    return result


def unflip(index, mask, count):
    if count & (count - 1):
        return lax.rem(index + count - mask, count)
    return flip(index, mask, count)


def kernel(
    n,
    per,
    features_hbm,
    gate_in_hbm,
    conv_weight_hbm,
    conv_bias_hbm,
    log_decay_hbm,
    step_size_hbm,
    gate_gain_hbm,
    w_out_hbm,
    boundaries_hbm,
    pad_vector_hbm,
    main_gain_hbm,
    w_gate_hbm,
    w_up_hbm,
    w_down_hbm,
    out,
    feat_x,
    feat_bc,
    halo_x,
    halo_bc,
    gate_in,
    conv_weight,
    conv_bias,
    log_decay,
    step_size,
    gate_gain,
    w_out,
    boundaries,
    pad_vector,
    main_gain,
    w_gate,
    w_up,
    w_down,
    xs,
    x_buf,
    bc_buf,
    dec,
    sbuf,
    rbuf,
    obuf,
    inbuf,
    base_out,
    coef_out,
    gated,
    block_base,
    block_coef,
    block_c,
    picked,
    own_half,
    enc,
    gath,
    own_rows,
    part,
    own_part,
    sums,
    last_part,
    last_sums,
    last_row,
    table,
    load_sem,
    core_send,
    core_recv,
    halo_send,
    halo_recv,
    dec_send,
    dec_recv,
    st1_send,
    st1_recv,
    st2_send,
    st2_recv,
    ag_send,
    ag_recv,
    rs_send,
    rs_recv,
    last_send,
    last_recv,
    ready,
):
    me = lax.axis_index("seq")
    chips = n // 2
    chip, core = lax.div(me, 2), lax.rem(me, 2)
    other = 1 - core
    partner = chip * 2 + other
    rows, half = feat_x.shape[1:]
    both = 2 * rows
    state_dim = feat_bc.shape[2] // 2
    inner = 2 * half
    channels = half + 2 * state_dim
    heads = log_decay.shape[1]
    head_dim = half // heads
    piece = state_dim // chips
    taps = conv_weight.shape[0]
    window = gath.shape[2]
    width = out.shape[1]

    barrier = pltpu.get_barrier_semaphore()
    end = chips - 1

    def tell(semaphore, who):
        pl.semaphore_signal(
            semaphore, inc=1, device_id={"seq": who}, device_id_type=pl.DeviceIdType.MESH
        )

    tell(barrier, partner)

    @pl.when(chip < end)
    def _():
        for q in range(chips):
            for k in range(2):

                @pl.when(chip != q)
                def _(q=q, k=k):
                    tell(barrier, 2 * q + k)

    def columns(which):
        return pl.ds(pl.multiple_of(which * half, half), half)

    def head_rows(which):
        return pl.ds(pl.multiple_of(which * heads, heads), heads)

    loads = {}

    def load(name, src, dst):
        c = pltpu.make_async_copy(src, dst, load_sem.at[len(loads)])
        c.start()
        loads[name] = c

    bc_columns = pl.ds(inner, 2 * state_dim)
    load("decay", log_decay_hbm.at[head_rows(core)], log_decay.at[core])
    load("step", step_size_hbm.at[head_rows(core)], step_size.at[core])
    load("x", features_hbm.at[:, columns(core)], feat_x.at[core])
    load("bc", features_hbm.at[:, bc_columns], feat_bc.at[core])
    load("taps", conv_weight_hbm, conv_weight)
    load("bias", conv_bias_hbm, conv_bias)
    load("bounds", boundaries_hbm, boundaries)
    load("gate_in", gate_in_hbm.at[:, columns(core)], gate_in.at[core])
    load("gate_gain", gate_gain_hbm, gate_gain)
    load("w_out", w_out_hbm, w_out)
    load("pad", pad_vector_hbm, pad_vector)
    load("main_gain", main_gain_hbm, main_gain)
    load("w_gate", w_gate_hbm, w_gate.at[core])
    load("w_up", w_up_hbm, w_up.at[core])
    load("w_down", w_down_hbm, w_down.at[core])

    def remote(src, dst, ssem, rsem, peer):
        return pltpu.make_async_remote_copy(
            src_ref=src,
            dst_ref=dst,
            send_sem=ssem,
            recv_sem=rsem,
            device_id={"seq": peer},
            device_id_type=pl.DeviceIdType.MESH,
        )

    def same_core(which):
        return which * 2 + core

    row_i = lax.broadcasted_iota(jnp.int32, (rows, rows), 0)
    col_i = lax.broadcasted_iota(jnp.int32, (rows, rows), 1)
    causal = row_i >= col_i
    upto = (row_i <= col_i).astype(F32).astype(BF16)
    hid = lax.rem(lax.broadcasted_iota(jnp.int32, (2 * heads, half), 0), heads) * head_dim
    lane = lax.broadcasted_iota(jnp.int32, (2 * heads, half), 1)
    onehot = ((lane >= hid) & (lane < hid + head_dim)).astype(F32).astype(BF16)
    lanes = lax.broadcasted_iota(jnp.int32, (heads, rows), 1)

    def expand(v):
        hi = v.astype(BF16).astype(F32)
        return mm(jnp.concatenate([hi, v - hi], axis=0).T.astype(BF16), onehot)

    def expand_each(values):
        packed = jnp.zeros((heads, rows), F32)
        for i, v in enumerate(values):
            packed = jnp.where(lanes == i, v, packed)
        return expand(packed)

    def summed(which):
        v = log_decay[which]
        parts = []
        for _ in range(3):
            parts.append(v.astype(BF16).astype(F32))
            v = v - parts[-1]
        sums = mm(jnp.concatenate(parts, axis=0).astype(BF16), upto)
        return sums[:heads] + sums[heads : 2 * heads] + sums[2 * heads :]

    def in_coefs(which, cum):
        mid = cum[:, rows // 2 : rows // 2 + 1]
        return expand(step_size[which] * jnp.exp(mid - cum))

    loads["decay"].wait()
    own_cum = summed(core)
    loads["step"].wait()
    own_coef = in_coefs(core, own_cum)

    @pl.when(chip < end)
    def _():
        pl.semaphore_wait(barrier, n - 3)

    @pl.when(chip == end)
    def _():
        pl.semaphore_wait(barrier, n - 1)
        for q in range(2 * end):
            tell(ready, q)

    exchange = {}

    def swap(name, src, dst):
        i = len(exchange)
        exchange[name] = remote(src, dst, core_send.at[i], core_recv.at[i], partner)
        exchange[name].start()

    halo_rows = pl.ds(rows - TILE, TILE)
    halos = []
    nxt = lax.rem(chip + 1, chips)
    for k in range(2):
        halos.append(
            remote(
                features_hbm.at[halo_rows, pl.ds(k * half, half)],
                halo_x,
                halo_send.at[2 * k],
                halo_recv.at[0],
                2 * nxt + k,
            )
        )
        halos.append(
            remote(
                features_hbm.at[halo_rows, bc_columns],
                halo_bc,
                halo_send.at[2 * k + 1],
                halo_recv.at[1],
                2 * nxt + k,
            )
        )

    @pl.when((core == 1) & (chip < end - 1))
    def _():
        for c in halos:
            c.start()

    swap("decay", log_decay_hbm.at[head_rows(other)], log_decay.at[core])
    swap("x", features_hbm.at[:, columns(other)], feat_x.at[core])
    swap("bc", features_hbm.at[:, bc_columns], feat_bc.at[core])
    swap("step", step_size_hbm.at[head_rows(other)], step_size.at[core])
    swap("gate_in", gate_in_hbm.at[:, columns(other)], gate_in.at[core])

    @pl.when(chip == 0)
    def _():
        halo_x[...] = jnp.zeros(halo_x.shape, BF16)
        halo_bc[...] = jnp.zeros(halo_bc.shape, BF16)

    def my_columns(v):
        mine = jnp.where(core == 0, v[:, :half], v[:, half:inner])
        return jnp.concatenate([mine, v[:, inner:]], axis=1)

    loads["taps"].wait()
    loads["bias"].wait()
    weight = my_columns(conv_weight[...])
    bias = my_columns(conv_bias[...].reshape(1, inner + 2 * state_dim))

    def convolved(which, first, count, coef):
        mixed = bias
        for k in range(taps):
            mixed = mixed + weight[k : k + 1] * xs[
                which, pl.ds(TILE - taps + 1 + first + k, count), :
            ]
        mixed = silu(mixed)
        x_new = (mixed[:, :half].astype(BF16).astype(F32) * coef).astype(BF16)
        x_buf[which, pl.ds(first, count), :] = x_new
        bc_buf[which, pl.ds(first, count), :] = mixed[:, half:].astype(BF16)
        b_new = mixed[:, half : half + state_dim]
        return mm(b_new.T.astype(BF16), x_new)

    def without_head(which, coef):
        xs[which, pl.ds(TILE, rows), :half] = feat_x[which].astype(F32)
        xs[which, pl.ds(TILE, rows), half:] = feat_bc[which].astype(F32)
        return convolved(which, TILE, rows - TILE, coef[TILE:])

    loads["x"].wait()
    loads["bc"].wait()
    own_state = without_head(core, own_coef)
    exchange["decay"].wait_recv()
    exchange["step"].wait_recv()
    their_cum = summed(other)
    their_coef = in_coefs(other, their_cum)

    def ordered(own, their):
        return jnp.where(core == 0, own, their), jnp.where(core == 0, their, own)

    cum = ordered(own_cum, their_cum)
    total = [c[:, rows - 1 :] for c in cum]
    mid = [c[:, rows // 2 : rows // 2 + 1] for c in cum]
    dec[chip] = jnp.broadcast_to(total[0] + total[1], dec.shape[1:])
    masks = range(1, chips)
    dec_copies = []
    for m in masks:
        q = flip(chip, m, chips)
        dec_copies.append(
            remote(dec.at[chip], dec.at[chip], dec_send.at[q], dec_recv.at[chip], same_core(q))
        )

    @pl.when(chip < end)
    def _():
        pl.semaphore_wait(ready, 2)
        for c in dec_copies:
            c.start()

    @pl.when((core == 1) & (chip == end - 1))
    def _():
        for c in halos:
            c.start()

    ends = expand_each(
        [
            jnp.exp(total[0] - mid[0]),
            jnp.exp(total[0] - mid[0] + total[1]),
            jnp.exp(total[1] - mid[1]),
            jnp.exp(mid[1]),
        ]
    )

    exchange["x"].wait_recv()
    exchange["bc"].wait_recv()
    their_state = without_head(other, their_coef)
    head_coef = ordered(own_coef[:TILE], their_coef[:TILE])
    states = ordered(own_state, their_state)
    xs[1, pl.ds(0, TILE), :half] = feat_x[0, rows - TILE :, :].astype(F32)
    xs[1, pl.ds(0, TILE), half:] = feat_bc[0, rows - TILE :, :].astype(F32)
    late = (states[1] + convolved(1, 0, TILE, head_coef[1])) * ends[2:3]

    @pl.when(chip > 0)
    def _():
        for i, dst in enumerate((halo_x, halo_bc)):
            remote(dst, dst, halo_send.at[i], halo_recv.at[i], partner).wait_recv()

    xs[0, pl.ds(0, TILE), :half] = halo_x[...].astype(F32)
    xs[0, pl.ds(0, TILE), half:] = halo_bc[...].astype(F32)
    state_a = states[0] + convolved(0, 0, TILE, head_coef[0])
    state = state_a * ends[1:2] + late
    part_lanes = half // SPLIT
    for j in range(chips):
        for h in range(SPLIT):
            sbuf[h * chips + j] = state[
                j * piece : (j + 1) * piece, h * part_lanes : (h + 1) * part_lanes
            ].astype(BF16)
    st1 = []
    for h in range(SPLIT):
        for m in masks:
            q = flip(chip, m, chips)
            at, to = h * chips + chip, h * chips + q
            st1.append(
                remote(sbuf.at[to], rbuf.at[at], st1_send.at[to], st1_recv.at[at], same_core(q))
            )

    @pl.when(chip < chips - 1)
    def _():
        for c in st1:
            c.start()

    swap("w_gate", w_gate_hbm, w_gate.at[core])
    swap("w_up", w_up_hbm, w_up.at[core])
    swap("w_down", w_down_hbm, w_down.at[core])
    for h in range(SPLIT):
        rbuf[h * chips + chip] = sbuf[h * chips + chip]

    loads["bounds"].wait()
    bnd = boundaries[...].reshape(1, boundaries.shape[0])

    def count(flags):
        return jnp.sum(flags.astype(F32), axis=1, keepdims=True).astype(jnp.int32)

    first_block = count(bnd < chip * both)
    end_block = count(bnd < (chip + 1) * both)

    def slots_of(pos):
        slot = count(bnd <= pos) - 1 - first_block
        return slot, jnp.where(slot < window - 1, slot, slot + 1)

    pos = chip * both + lax.broadcasted_iota(jnp.int32, (both, 1), 0)
    starts = count(bnd == pos) > 0
    slot, entry = slots_of(pos)
    is_last = slot == end_block - 1 - first_block
    at = lax.broadcasted_iota(jnp.int32, (both, 2 * window), 1)
    at = jnp.where(at < window, at + core * window, at + (other - 1) * window)
    chosen = (entry == at) | ((at == window - 1) & is_last)
    pick = jnp.where(chosen & starts, 1.0, 0.0).T.astype(BF16)

    for k in range(end):

        @pl.when(chip != k)
        def _(k=k):
            remote(dec.at[k], dec.at[k], dec_send.at[k], dec_recv.at[k], partner).wait_recv()

    decays = jnp.exp(expand_each([dec[k, :, :1] for k in range(end)])[:chips])

    def carry(h, k):
        at, to = h * chips + chip, h * chips + k
        return remote(obuf.at[to], inbuf.at[at], st2_send.at[to], st2_recv.at[at], same_core(k))

    for h in range(SPLIT):
        for k in range(end):

            @pl.when(chip != k)
            def _(at=h * chips + k):
                remote(
                    rbuf.at[at], rbuf.at[at], st1_send.at[at], st1_recv.at[at], partner
                ).wait_recv()

        before = jnp.zeros((piece, part_lanes), F32)
        for k in range(end):
            decay = decays[k : k + 1, h * part_lanes : (h + 1) * part_lanes]
            before = before * decay + rbuf[h * chips + k].astype(F32)
            obuf[h * chips + k + 1] = before.astype(BF16)
        for k in range(1, chips):

            @pl.when(chip != k)
            def _(h=h, k=k):
                carry(h, k).start()

    loads["gate_in"].wait()
    exchange["gate_in"].wait_recv()
    state_mid = (state_a * ends[0:1]).astype(BF16)
    for j in range(2):
        at = pl.ds(j * rows, rows)
        b_part = bc_buf[j, :, :state_dim]
        c_part = bc_buf[j, :, state_dim:]
        prod = lax.dot_general(
            c_part, b_part, (((1,), (1,)), ((), ())), preferred_element_type=F32
        )
        local = mm(jnp.where(causal, prod, 0.0).astype(BF16), x_buf[j])
        if j == 1:
            local = local + mm(c_part, state_mid) * ends[3:4]
        gate = silu(gate_in[j].astype(F32))
        base_out[at, :] = local * expand(jnp.exp(cum[j] - mid[j])) * gate
        start = cum[j] if j == 0 else cum[j] + total[0]
        coef_out[at, :] = expand(jnp.exp(start)) * gate

    def pick_exact(v):
        hi = v.astype(BF16)
        return mm(pick, hi) + mm(pick, (v - hi.astype(F32)).astype(BF16))

    block_base[...] = pick_exact(base_out[...])
    block_coef[...] = pick_exact(coef_out[...])
    c_all = bc_buf[:, :, state_dim:].reshape(both, state_dim)
    block_c[...] = mm(pick, c_all).astype(BF16)
    slot, entry = slots_of(me * rows + lax.broadcasted_iota(jnp.int32, (rows, 1), 0))
    entry = jnp.where(slot < 0, window - 1, entry)
    spread = jnp.where(
        entry == lax.broadcasted_iota(jnp.int32, (rows, 2 * window), 1), 1.0, 0.0
    ).astype(BF16)

    @pl.when(chip == 0)
    def _():
        inbuf[...] = jnp.zeros(inbuf.shape, BF16)

    states_in = []
    for h in range(SPLIT):

        @pl.when(chip > 0)
        def _(h=h):
            inbuf[h * chips + chip] = obuf[h * chips + chip]
            for m in masks:
                at = h * chips + unflip(chip, m, chips)
                remote(
                    inbuf.at[at], inbuf.at[at], st2_send.at[at], st2_recv.at[at], partner
                ).wait_recv()

        parts = inbuf[h * chips : (h + 1) * chips]
        if piece % TILE == 0:
            states_in.append(parts.reshape(state_dim, part_lanes))
        else:
            parts = [parts[k].astype(F32) for k in range(chips)]
            states_in.append(jnp.concatenate(parts, axis=0).astype(BF16))

    def carried_by(c):
        return jnp.concatenate([mm(c, state) for state in states_in], axis=1)

    carried = carried_by(block_c[...])
    rows_out = (block_base[...] + carried * block_coef[...]).astype(BF16)
    gath[chip, core] = rows_out[:window]
    picked[...] = rows_out[window:]
    ag = []
    sends = [m for m in (3, 1, 2) if m < chips] + list(range(4, chips))
    for m in sends:
        q = flip(chip, m, chips)
        for i, (src, to) in enumerate(
            ((gath.at[chip, core], same_core(q)), (picked, 2 * q + other))
        ):
            c = remote(src, gath.at[chip, core], ag_send.at[2 * q + i], ag_recv.at[me], to)
            c.start()
            ag.append(c)
    swap("picked", picked, gath.at[chip, core])

    loads["gate_gain"].wait()
    loads["w_out"].wait()

    def project(pairs):
        v = jnp.concatenate(
            [
                jnp.concatenate([p[0].astype(F32), p[1].astype(F32)], axis=1)
                for p in pairs
            ],
            axis=0,
        )
        scale = lax.rsqrt(jnp.mean(v * v, axis=1, keepdims=True) + EPSILON)
        gain = gate_gain[...].reshape(1, inner)
        gained = (v * gain).astype(BF16)
        return (mm_rows(gained, w_out[...])[: v.shape[0]] * scale).astype(BF16)


    loads["pad"].wait()
    loads["main_gain"].wait()
    main_width = main_gain.shape[0]
    main = main_gain[...].reshape(1, main_width)
    pad = pad_vector[...].astype(F32).reshape(1, main_width - width)
    pad_sum = jnp.sum(pad * pad, axis=1, keepdims=True)
    pad_gain = pad * main[:, width:]

    def hidden_of(rows_in):
        v = rows_in.astype(F32)
        mean = (jnp.sum(v * v, axis=1, keepdims=True) + pad_sum) / main_width
        scale = lax.rsqrt(mean + EPSILON)
        act = (v * main[:, :width]).astype(BF16)
        short = -v.shape[0] % FULL
        if short:
            act = jnp.concatenate([act, jnp.zeros((short, width), BF16)], axis=0)
            scale = jnp.concatenate([scale, jnp.zeros((short, 1), F32)], axis=0)
        hidden = []
        for k in range(2):
            gate = (mm(act, w_gate[k, :width, :]) + pad_gate[k]) * scale
            up = (mm(act, w_up[k, :width, :]) + pad_up[k]) * scale
            hidden.append((silu(gate) * up).astype(BF16))
        return hidden

    span = width // 2

    def part_of(c):
        return slice(c * span, (c + 1) * span)

    def down(hidden, c):
        return mm(hidden[0], w_down[0, :, part_of(c)]) + mm(hidden[1], w_down[1, :, part_of(c)])

    def row_of(parts, at):
        return jnp.concatenate([p[at : at + 1] for p in parts], axis=1)

    for name in ("w_gate", "w_up", "w_down"):
        loads[name].wait()
        exchange[name].wait_recv()
    pad_rows = jnp.broadcast_to(pad_gain, (TILE, main_width - width)).astype(BF16)
    pad_gate = [mm(pad_rows, w_gate[k, width:, :])[:1] for k in range(2)]
    pad_up = [mm(pad_rows, w_up[k, width:, :])[:1] for k in range(2)]

    def send_last(source):
        dest = lax.rem(source + 1, chips)
        c = remote(
            last_part.at[source],
            last_sums.at[chip],
            last_send.at[source],
            last_recv.at[chip],
            2 * dest,
        )
        return c, (core == 0) & (source < chips - 1) & (dest != chip)

    def start_last(source):
        c, needed = send_last(source)

        @pl.when(needed)
        def _():
            c.start()

    rs = []
    groups = [sends[:1], sends[1:3], *[sends[i : i + 3] for i in range(3, len(sends), 3)]]
    for group in groups:
        sources = [unflip(chip, m, chips) for m in group]
        for q in sources:
            for k in range(2):
                ref = gath.at[q, k]
                remote(ref, ref, ag_send.at[2 * q + k], ag_recv.at[2 * q + k], partner).wait_recv()
        blocks = project([gath.at[q] for q in sources])
        hidden = hidden_of(blocks)
        downs = []
        for c in range(2):
            downs.append(down(hidden, c))
            for i, q in enumerate(sources):
                part[c, q] = downs[c][i * window : (i + 1) * window].astype(BF16)
                at, to = c * chips + chip, c * chips + q
                copy = remote(
                    part.at[c, q], sums.at[c, chip], rs_send.at[to], rs_recv.at[at], same_core(q)
                )
                copy.start()
                rs.append(copy)
        for i, q in enumerate(sources):
            last_part[q] = row_of(downs, (i + 1) * window - 1)
            last_row[q] = blocks[(i + 1) * window - TILE : (i + 1) * window].astype(F32)[TILE - 1 :]
            start_last(q)

    gated[...] = (base_out[...] + carried_by(c_all) * coef_out[...]).astype(BF16)
    their_rows = pl.ds(pl.multiple_of(other * rows, rows), rows)
    my_rows = pl.ds(pl.multiple_of(core * rows, rows), rows)
    swap("gated", gated.at[their_rows], own_half.at[core])
    own_half[core] = gated[my_rows, :]
    exchange["picked"].wait_recv()
    own_rows[...] = project([gath.at[chip]])
    hidden = hidden_of(own_rows[...])
    downs = [down(hidden, c) for c in range(2)]
    for c in range(2):
        own_part[c] = downs[c][:window]
    last_part[chip] = row_of(downs, window - 1)
    start_last(chip)
    exchange["gated"].wait_recv()
    enc[...] = project([own_half])
    prev = lax.rem(chip + chips - 1, chips)
    last = last_row[prev] + last_part[prev]
    for m in masks:
        q = unflip(chip, m, chips)

        @pl.when((core == 0) & (chip > 0))
        def _(q=q):
            remote(
                last_sums.at[q], last_sums.at[q], last_send.at[q], last_recv.at[q], partner
            ).wait_recv()

        last = last + last_sums[q]
    row = lax.broadcasted_iota(jnp.int32, (window, 1), 0)
    from_before = (row == window - 1) & (core == 0) & (chip > 0)
    for c in range(2):
        result = own_rows[:, part_of(c)].astype(F32) + own_part[c]
        for m in masks:
            q = unflip(chip, m, chips)
            at, ref = c * chips + q, sums.at[c, q]
            remote(ref, ref, rs_send.at[at], rs_recv.at[at], partner).wait_recv()
            result = result + sums[c, q].astype(F32)
        table[c, core] = jnp.where(from_before, last[:, part_of(c)], result).astype(BF16)
        swap(f"table {c}", table.at[c, core], table.at[c, core])
    for c in range(2):
        exchange[f"table {c}"].wait_recv()
        expanded = mm(spread, table[c].reshape(2 * window, span))
        out[:, part_of(c)] = (enc[:, part_of(c)].astype(F32) + expanded).astype(BF16)

    for c in [*exchange.values(), *ag, *rs]:
        c.wait_send()

    @pl.when((core == 1) & (chip < chips - 1))
    def _():
        for c in halos:
            c.wait_send()

    @pl.when(chip < chips - 1)
    def _():
        for c in [*dec_copies, *st1]:
            c.wait_send()

    for h in range(SPLIT):
        for k in range(1, chips):

            @pl.when(chip != k)
            def _(h=h, k=k):
                carry(h, k).wait_send()

    for k in range(chips - 1):
        c, needed = send_last(k)

        @pl.when(needed)
        def _(c=c):
            c.wait_send()


def per_device(
    n,
    features,
    gate_in,
    conv_weight,
    conv_bias,
    log_decay,
    step_size,
    gate_gain,
    w_out,
    boundaries,
    pad_vector,
    main_gain,
    w_gate,
    w_up,
    w_down,
):
    rows, channels = features.shape
    inner = gate_in.shape[1]
    heads = log_decay.shape[1] // 2
    width = w_out.shape[1]
    bc = channels - inner
    half = inner // 2
    chips = n // 2
    piece = bc // 2 // chips
    per = boundaries.shape[0] // n
    window = 3 * per // 2
    vmem = pl.BlockSpec(memory_space=pltpu.VMEM)
    hbm = pl.BlockSpec(memory_space=pl.ANY)
    dma = pltpu.SemaphoreType.DMA
    args = (
        features,
        gate_in,
        conv_weight,
        conv_bias,
        log_decay.T,
        step_size.T,
        gate_gain,
        w_out,
        boundaries,
        pad_vector,
        main_gain,
        w_gate,
        w_up,
        w_down,
    )

    def like(a):
        return pltpu.VMEM(a.shape, a.dtype)

    def twice(a):
        return pltpu.VMEM((2, *a.shape), a.dtype)

    states = pltpu.VMEM((SPLIT * chips, piece, half // SPLIT), BF16)
    return pl.pallas_call(
        functools.partial(kernel, n, per),
        out_shape=pltpu.VMEM((rows, width), BF16),
        in_specs=[hbm] * len(args),
        out_specs=vmem,
        scratch_shapes=[
            pltpu.VMEM((2, rows, half), BF16),
            pltpu.VMEM((2, rows, bc), BF16),
            pltpu.VMEM((TILE, half), BF16),
            pltpu.VMEM((TILE, bc), BF16),
            pltpu.VMEM((2, rows, half), BF16),
            like(conv_weight),
            like(conv_bias),
            pltpu.VMEM((2, heads, rows), F32),
            pltpu.VMEM((2, heads, rows), F32),
            like(gate_gain),
            like(w_out),
            like(boundaries),
            like(pad_vector),
            like(main_gain),
            twice(w_gate),
            twice(w_up),
            twice(w_down),
            pltpu.VMEM((2, TILE + rows, half + bc), F32),
            pltpu.VMEM((2, rows, half), BF16),
            pltpu.VMEM((2, rows, bc), BF16),
            pltpu.VMEM((chips, heads, 128), F32),
            states,
            states,
            states,
            states,
            pltpu.VMEM((2 * rows, half), F32),
            pltpu.VMEM((2 * rows, half), F32),
            pltpu.VMEM((2 * rows, half), BF16),
            pltpu.VMEM((2 * window, half), F32),
            pltpu.VMEM((2 * window, half), F32),
            pltpu.VMEM((2 * window, bc // 2), BF16),
            pltpu.VMEM((window, half), BF16),
            pltpu.VMEM((2, rows, half), BF16),
            pltpu.VMEM((rows, width), BF16),
            pltpu.VMEM((chips, 2, window, half), BF16),
            pltpu.VMEM((window, width), BF16),
            pltpu.VMEM((2, chips, window, width // 2), BF16),
            pltpu.VMEM((2, window, width // 2), F32),
            pltpu.VMEM((2, chips, window, width // 2), BF16),
            pltpu.VMEM((chips, 1, width), F32),
            pltpu.VMEM((chips, 1, width), F32),
            pltpu.VMEM((chips, 1, width), F32),
            pltpu.VMEM((2, 2, window, width // 2), BF16),
            dma((16,)),
            dma((16,)),
            dma((16,)),
            dma((4,)),
            dma((2,)),
            dma((chips,)),
            dma((chips,)),
            *[dma((SPLIT * chips,)) for _ in range(4)],
            dma((n,)),
            dma((n,)),
            dma((n,)),
            dma((n,)),
            dma((chips,)),
            dma((chips,)),
            pltpu.SemaphoreType.REGULAR,
        ],
        compiler_params=pltpu.CompilerParams(collective_id=0, has_side_effects=True),
    )(*args)


def solution(mesh):
    in_specs = (
        P(("doc", "seq"), None),
        P(("doc", "seq"), None),
        P(),
        P(),
        P(("doc", "seq"), None),
        P(("doc", "seq"), None),
        P(),
        P(),
        P("doc"),
        P(),
        P(),
        P(None, "seq"),
        P(None, "seq"),
        P("seq", None),
    )
    out_specs = P(("doc", "seq"), None)
    return jax.shard_map(
        functools.partial(per_device, mesh.shape["seq"]),
        mesh=mesh,
        in_specs=in_specs,
        out_specs=out_specs,
        check_vma=False,
    )
```

```python
import functools

import jax
import jax.numpy as jnp
from jax import lax
from jax.experimental import pallas as pl
from jax.experimental.pallas import tpu as pltpu
from jax.sharding import PartitionSpec as P

EPSILON = 1e-05
TILE = 16
FULL = 128
SPLIT = 2
F32 = jnp.float32
BF16 = jnp.bfloat16


def mm(a, b):
    return jnp.dot(a, b, preferred_element_type=F32)


def mm_rows(a, w):
    count = a.shape[0]
    short = -count % FULL
    if short:
        a = jnp.concatenate([a, jnp.zeros((short, a.shape[1]), a.dtype)], axis=0)
    return mm(a, w)


def silu(v):
    return 0.5 * v * (1.0 + jnp.tanh(0.5 * v))


def flip(index, mask, count):
    if count & (count - 1):
        return lax.rem(index + mask, count)
    bit, result = 1, index
    while bit < count:
        if mask & bit:
            result = result + (1 - 2 * lax.rem(lax.div(index, bit), 2)) * bit
        bit *= 2
    return result


def unflip(index, mask, count):
    if count & (count - 1):
        return lax.rem(index + count - mask, count)
    return flip(index, mask, count)


def kernel(
    n,
    per,
    features_hbm,
    gate_in_hbm,
    conv_weight_hbm,
    conv_bias_hbm,
    log_decay_hbm,
    step_size_hbm,
    gate_gain_hbm,
    w_out_hbm,
    boundaries_hbm,
    pad_vector_hbm,
    main_gain_hbm,
    w_gate_hbm,
    w_up_hbm,
    w_down_hbm,
    out,
    feat_x,
    feat_bc,
    halo_x,
    halo_bc,
    gate_in,
    conv_weight,
    conv_bias,
    log_decay,
    step_size,
    gate_gain,
    w_out,
    boundaries,
    pad_vector,
    main_gain,
    w_gate,
    w_up,
    w_down,
    xs,
    x_buf,
    bc_buf,
    dec,
    sbuf,
    rbuf,
    obuf,
    inbuf,
    base_out,
    coef_out,
    gated,
    block_base,
    block_coef,
    block_c,
    picked,
    own_half,
    enc,
    gath,
    own_rows,
    part,
    own_part,
    sums,
    last_part,
    last_sums,
    last_row,
    table,
    load_sem,
    core_send,
    core_recv,
    halo_send,
    halo_recv,
    dec_send,
    dec_recv,
    st1_send,
    st1_recv,
    st2_send,
    st2_recv,
    ag_send,
    ag_recv,
    rs_send,
    rs_recv,
    last_send,
    last_recv,
    ready,
):
    me = lax.axis_index("seq")
    chips = n // 2
    chip, core = lax.div(me, 2), lax.rem(me, 2)
    other = 1 - core
    partner = chip * 2 + other
    rows, half = feat_x.shape[1:]
    both = 2 * rows
    state_dim = feat_bc.shape[2] // 2
    inner = 2 * half
    channels = half + 2 * state_dim
    heads = log_decay.shape[1]
    head_dim = half // heads
    piece = state_dim // chips
    taps = conv_weight.shape[0]
    window = gath.shape[2]
    width = out.shape[1]

    barrier = pltpu.get_barrier_semaphore()
    end = chips - 1

    def tell(semaphore, who):
        pl.semaphore_signal(
            semaphore, inc=1, device_id={"seq": who}, device_id_type=pl.DeviceIdType.MESH
        )

    tell(barrier, partner)

    @pl.when(chip < end)
    def _():
        for q in range(chips):
            for k in range(2):

                @pl.when(chip != q)
                def _(q=q, k=k):
                    tell(barrier, 2 * q + k)

    def columns(which):
        return pl.ds(pl.multiple_of(which * half, half), half)

    def head_rows(which):
        return pl.ds(pl.multiple_of(which * heads, heads), heads)

    loads = {}

    def load(name, src, dst):
        c = pltpu.make_async_copy(src, dst, load_sem.at[len(loads)])
        c.start()
        loads[name] = c

    bc_columns = pl.ds(inner, 2 * state_dim)
    load("decay", log_decay_hbm.at[head_rows(core)], log_decay.at[core])
    load("step", step_size_hbm.at[head_rows(core)], step_size.at[core])
    load("x", features_hbm.at[:, columns(core)], feat_x.at[core])
    load("bc", features_hbm.at[:, bc_columns], feat_bc.at[core])
    load("taps", conv_weight_hbm, conv_weight)
    load("bias", conv_bias_hbm, conv_bias)
    load("bounds", boundaries_hbm, boundaries)
    load("gate_in", gate_in_hbm.at[:, columns(core)], gate_in.at[core])
    load("gate_gain", gate_gain_hbm, gate_gain)
    load("w_out", w_out_hbm, w_out)
    load("pad", pad_vector_hbm, pad_vector)
    load("main_gain", main_gain_hbm, main_gain)
    load("w_gate", w_gate_hbm, w_gate.at[core])
    load("w_up", w_up_hbm, w_up.at[core])
    load("w_down", w_down_hbm, w_down.at[core])

    def remote(src, dst, ssem, rsem, peer):
        return pltpu.make_async_remote_copy(
            src_ref=src,
            dst_ref=dst,
            send_sem=ssem,
            recv_sem=rsem,
            device_id={"seq": peer},
            device_id_type=pl.DeviceIdType.MESH,
        )

    def same_core(which):
        return which * 2 + core

    row_i = lax.broadcasted_iota(jnp.int32, (rows, rows), 0)
    col_i = lax.broadcasted_iota(jnp.int32, (rows, rows), 1)
    causal = row_i >= col_i
    upto = (row_i <= col_i).astype(F32).astype(BF16)
    hid = lax.rem(lax.broadcasted_iota(jnp.int32, (2 * heads, half), 0), heads) * head_dim
    lane = lax.broadcasted_iota(jnp.int32, (2 * heads, half), 1)
    onehot = ((lane >= hid) & (lane < hid + head_dim)).astype(F32).astype(BF16)
    lanes = lax.broadcasted_iota(jnp.int32, (heads, rows), 1)

    def expand(v):
        hi = v.astype(BF16).astype(F32)
        return mm(jnp.concatenate([hi, v - hi], axis=0).T.astype(BF16), onehot)

    def expand_each(values):
        packed = jnp.zeros((heads, rows), F32)
        for i, v in enumerate(values):
            packed = jnp.where(lanes == i, v, packed)
        return expand(packed)

    def summed(which):
        v = log_decay[which]
        parts = []
        for _ in range(3):
            parts.append(v.astype(BF16).astype(F32))
            v = v - parts[-1]
        sums = mm(jnp.concatenate(parts, axis=0).astype(BF16), upto)
        return sums[:heads] + sums[heads : 2 * heads] + sums[2 * heads :]

    def in_coefs(which, cum):
        mid = cum[:, rows // 2 : rows // 2 + 1]
        return expand(step_size[which] * jnp.exp(mid - cum))


    @pl.when(chip < end)
    def _():
        pl.semaphore_wait(barrier, n - 3)

    @pl.when(chip == end)
    def _():
        pl.semaphore_wait(barrier, n - 1)
        for q in range(2 * end):
            tell(ready, q)

    exchange = {}

    def swap(name, src, dst):
        i = len(exchange)
        exchange[name] = remote(src, dst, core_send.at[i], core_recv.at[i], partner)
        exchange[name].start()

    halo_rows = pl.ds(rows - TILE, TILE)
    halos = []
    nxt = lax.rem(chip + 1, chips)
    for k in range(2):
        halos.append(
            remote(
                features_hbm.at[halo_rows, pl.ds(k * half, half)],
                halo_x,
                halo_send.at[2 * k],
                halo_recv.at[0],
                2 * nxt + k,
            )
        )
        halos.append(
            remote(
                features_hbm.at[halo_rows, bc_columns],
                halo_bc,
                halo_send.at[2 * k + 1],
                halo_recv.at[1],
                2 * nxt + k,
            )
        )

    @pl.when((core == 1) & (chip < end - 1))
    def _():
        for c in halos:
            c.start()

    swap("decay", log_decay_hbm.at[head_rows(other)], log_decay.at[core])
    swap("x", features_hbm.at[:, columns(other)], feat_x.at[core])
    swap("bc", features_hbm.at[:, bc_columns], feat_bc.at[core])
    swap("step", step_size_hbm.at[head_rows(other)], step_size.at[core])
    swap("gate_in", gate_in_hbm.at[:, columns(other)], gate_in.at[core])
    loads["decay"].wait()
    own_cum = summed(core)
    loads["step"].wait()
    own_coef = in_coefs(core, own_cum)

    @pl.when(chip == 0)
    def _():
        halo_x[...] = jnp.zeros(halo_x.shape, BF16)
        halo_bc[...] = jnp.zeros(halo_bc.shape, BF16)

    def my_columns(v):
        mine = jnp.where(core == 0, v[:, :half], v[:, half:inner])
        return jnp.concatenate([mine, v[:, inner:]], axis=1)

    loads["taps"].wait()
    loads["bias"].wait()
    weight = my_columns(conv_weight[...])
    bias = my_columns(conv_bias[...].reshape(1, inner + 2 * state_dim))

    def convolved(which, first, count, coef):
        mixed = bias
        for k in range(taps):
            mixed = mixed + weight[k : k + 1] * xs[
                which, pl.ds(TILE - taps + 1 + first + k, count), :
            ]
        mixed = silu(mixed)
        x_new = (mixed[:, :half].astype(BF16).astype(F32) * coef).astype(BF16)
        x_buf[which, pl.ds(first, count), :] = x_new
        bc_buf[which, pl.ds(first, count), :] = mixed[:, half:].astype(BF16)
        b_new = mixed[:, half : half + state_dim]
        return mm(b_new.T.astype(BF16), x_new)

    def without_head(which, coef):
        xs[which, pl.ds(TILE, rows), :half] = feat_x[which].astype(F32)
        xs[which, pl.ds(TILE, rows), half:] = feat_bc[which].astype(F32)
        return convolved(which, TILE, rows - TILE, coef[TILE:])

    loads["x"].wait()
    loads["bc"].wait()
    own_state = without_head(core, own_coef)
    exchange["decay"].wait_recv()
    exchange["step"].wait_recv()
    their_cum = summed(other)
    their_coef = in_coefs(other, their_cum)

    def ordered(own, their):
        return jnp.where(core == 0, own, their), jnp.where(core == 0, their, own)

    cum = ordered(own_cum, their_cum)
    total = [c[:, rows - 1 :] for c in cum]
    mid = [c[:, rows // 2 : rows // 2 + 1] for c in cum]
    dec[chip] = jnp.broadcast_to(total[0] + total[1], dec.shape[1:])
    masks = range(1, chips)
    dec_copies = []
    for m in masks:
        q = flip(chip, m, chips)
        dec_copies.append(
            remote(dec.at[chip], dec.at[chip], dec_send.at[q], dec_recv.at[chip], same_core(q))
        )

    @pl.when(chip < end)
    def _():
        pl.semaphore_wait(ready, 2)
        for c in dec_copies:
            c.start()

    @pl.when((core == 1) & (chip == end - 1))
    def _():
        for c in halos:
            c.start()

    ends = expand_each(
        [
            jnp.exp(total[0] - mid[0]),
            jnp.exp(total[0] - mid[0] + total[1]),
            jnp.exp(total[1] - mid[1]),
            jnp.exp(mid[1]),
        ]
    )

    exchange["x"].wait_recv()
    exchange["bc"].wait_recv()
    their_state = without_head(other, their_coef)
    head_coef = ordered(own_coef[:TILE], their_coef[:TILE])
    states = ordered(own_state, their_state)
    xs[1, pl.ds(0, TILE), :half] = feat_x[0, rows - TILE :, :].astype(F32)
    xs[1, pl.ds(0, TILE), half:] = feat_bc[0, rows - TILE :, :].astype(F32)
    late = (states[1] + convolved(1, 0, TILE, head_coef[1])) * ends[2:3]

    @pl.when(chip > 0)
    def _():
        for i, dst in enumerate((halo_x, halo_bc)):
            remote(dst, dst, halo_send.at[i], halo_recv.at[i], partner).wait_recv()

    xs[0, pl.ds(0, TILE), :half] = halo_x[...].astype(F32)
    xs[0, pl.ds(0, TILE), half:] = halo_bc[...].astype(F32)
    state_a = states[0] + convolved(0, 0, TILE, head_coef[0])
    state = state_a * ends[1:2] + late
    part_lanes = half // SPLIT
    for j in range(chips):
        for h in range(SPLIT):
            sbuf[h * chips + j] = state[
                j * piece : (j + 1) * piece, h * part_lanes : (h + 1) * part_lanes
            ].astype(BF16)
    st1 = []
    for h in range(SPLIT):
        for m in masks:
            q = flip(chip, m, chips)
            at, to = h * chips + chip, h * chips + q
            st1.append(
                remote(sbuf.at[to], rbuf.at[at], st1_send.at[to], st1_recv.at[at], same_core(q))
            )

    @pl.when(chip < chips - 1)
    def _():
        for c in st1:
            c.start()

    swap("w_gate", w_gate_hbm, w_gate.at[core])
    swap("w_up", w_up_hbm, w_up.at[core])
    swap("w_down", w_down_hbm, w_down.at[core])
    for h in range(SPLIT):
        rbuf[h * chips + chip] = sbuf[h * chips + chip]

    loads["bounds"].wait()
    bnd = boundaries[...].reshape(1, boundaries.shape[0])

    def count(flags):
        return jnp.sum(flags.astype(F32), axis=1, keepdims=True).astype(jnp.int32)

    first_block = count(bnd < chip * both)
    end_block = count(bnd < (chip + 1) * both)

    def slots_of(pos):
        slot = count(bnd <= pos) - 1 - first_block
        return slot, jnp.where(slot < window - 1, slot, slot + 1)

    pos = chip * both + lax.broadcasted_iota(jnp.int32, (both, 1), 0)
    starts = count(bnd == pos) > 0
    slot, entry = slots_of(pos)
    is_last = slot == end_block - 1 - first_block
    at = lax.broadcasted_iota(jnp.int32, (both, 2 * window), 1)
    at = jnp.where(at < window, at + core * window, at + (other - 1) * window)
    chosen = (entry == at) | ((at == window - 1) & is_last)
    pick = jnp.where(chosen & starts, 1.0, 0.0).T.astype(BF16)

    for k in range(end):

        @pl.when(chip != k)
        def _(k=k):
            remote(dec.at[k], dec.at[k], dec_send.at[k], dec_recv.at[k], partner).wait_recv()

    decays = jnp.exp(expand_each([dec[k, :, :1] for k in range(end)])[:chips])

    def carry(h, k):
        at, to = h * chips + chip, h * chips + k
        return remote(obuf.at[to], inbuf.at[at], st2_send.at[to], st2_recv.at[at], same_core(k))

    for h in range(SPLIT):
        for k in range(end):

            @pl.when(chip != k)
            def _(at=h * chips + k):
                remote(
                    rbuf.at[at], rbuf.at[at], st1_send.at[at], st1_recv.at[at], partner
                ).wait_recv()

        before = jnp.zeros((piece, part_lanes), F32)
        for k in range(end):
            decay = decays[k : k + 1, h * part_lanes : (h + 1) * part_lanes]
            before = before * decay + rbuf[h * chips + k].astype(F32)
            obuf[h * chips + k + 1] = before.astype(BF16)
        for k in range(1, chips):

            @pl.when(chip != k)
            def _(h=h, k=k):
                carry(h, k).start()

    loads["gate_in"].wait()
    exchange["gate_in"].wait_recv()
    state_mid = (state_a * ends[0:1]).astype(BF16)
    for j in range(2):
        at = pl.ds(j * rows, rows)
        b_part = bc_buf[j, :, :state_dim]
        c_part = bc_buf[j, :, state_dim:]
        prod = lax.dot_general(
            c_part, b_part, (((1,), (1,)), ((), ())), preferred_element_type=F32
        )
        local = mm(jnp.where(causal, prod, 0.0).astype(BF16), x_buf[j])
        if j == 1:
            local = local + mm(c_part, state_mid) * ends[3:4]
        gate = silu(gate_in[j].astype(F32))
        base_out[at, :] = local * expand(jnp.exp(cum[j] - mid[j])) * gate
        start = cum[j] if j == 0 else cum[j] + total[0]
        coef_out[at, :] = expand(jnp.exp(start)) * gate

    def pick_exact(v):
        hi = v.astype(BF16)
        return mm(pick, hi) + mm(pick, (v - hi.astype(F32)).astype(BF16))

    block_base[...] = pick_exact(base_out[...])
    block_coef[...] = pick_exact(coef_out[...])
    c_all = bc_buf[:, :, state_dim:].reshape(both, state_dim)
    block_c[...] = mm(pick, c_all).astype(BF16)
    slot, entry = slots_of(me * rows + lax.broadcasted_iota(jnp.int32, (rows, 1), 0))
    entry = jnp.where(slot < 0, window - 1, entry)
    spread = jnp.where(
        entry == lax.broadcasted_iota(jnp.int32, (rows, 2 * window), 1), 1.0, 0.0
    ).astype(BF16)

    @pl.when(chip == 0)
    def _():
        inbuf[...] = jnp.zeros(inbuf.shape, BF16)

    states_in = []
    for h in range(SPLIT):

        @pl.when(chip > 0)
        def _(h=h):
            inbuf[h * chips + chip] = obuf[h * chips + chip]
            for m in masks:
                at = h * chips + unflip(chip, m, chips)
                remote(
                    inbuf.at[at], inbuf.at[at], st2_send.at[at], st2_recv.at[at], partner
                ).wait_recv()

        parts = inbuf[h * chips : (h + 1) * chips]
        if piece % TILE == 0:
            states_in.append(parts.reshape(state_dim, part_lanes))
        else:
            parts = [parts[k].astype(F32) for k in range(chips)]
            states_in.append(jnp.concatenate(parts, axis=0).astype(BF16))

    def carried_by(c):
        return jnp.concatenate([mm(c, state) for state in states_in], axis=1)

    carried = carried_by(block_c[...])
    rows_out = (block_base[...] + carried * block_coef[...]).astype(BF16)
    gath[chip, core] = rows_out[:window]
    picked[...] = rows_out[window:]
    ag = []
    sends = [m for m in (3, 1, 2) if m < chips] + list(range(4, chips))
    for m in sends:
        q = flip(chip, m, chips)
        for i, (src, to) in enumerate(
            ((gath.at[chip, core], same_core(q)), (picked, 2 * q + other))
        ):
            c = remote(src, gath.at[chip, core], ag_send.at[2 * q + i], ag_recv.at[me], to)
            c.start()
            ag.append(c)
    swap("picked", picked, gath.at[chip, core])

    loads["gate_gain"].wait()
    loads["w_out"].wait()

    def project(pairs):
        v = jnp.concatenate(
            [
                jnp.concatenate([p[0].astype(F32), p[1].astype(F32)], axis=1)
                for p in pairs
            ],
            axis=0,
        )
        scale = lax.rsqrt(jnp.mean(v * v, axis=1, keepdims=True) + EPSILON)
        gain = gate_gain[...].reshape(1, inner)
        gained = (v * gain).astype(BF16)
        return (mm_rows(gained, w_out[...])[: v.shape[0]] * scale).astype(BF16)


    loads["pad"].wait()
    loads["main_gain"].wait()
    main_width = main_gain.shape[0]
    main = main_gain[...].reshape(1, main_width)
    pad = pad_vector[...].astype(F32).reshape(1, main_width - width)
    pad_sum = jnp.sum(pad * pad, axis=1, keepdims=True)
    pad_gain = pad * main[:, width:]

    def hidden_of(rows_in):
        v = rows_in.astype(F32)
        mean = (jnp.sum(v * v, axis=1, keepdims=True) + pad_sum) / main_width
        scale = lax.rsqrt(mean + EPSILON)
        act = (v * main[:, :width]).astype(BF16)
        short = -v.shape[0] % FULL
        if short:
            act = jnp.concatenate([act, jnp.zeros((short, width), BF16)], axis=0)
            scale = jnp.concatenate([scale, jnp.zeros((short, 1), F32)], axis=0)
        hidden = []
        for k in range(2):
            gate = (mm(act, w_gate[k, :width, :]) + pad_gate[k]) * scale
            up = (mm(act, w_up[k, :width, :]) + pad_up[k]) * scale
            hidden.append((silu(gate) * up).astype(BF16))
        return hidden

    span = width // 2

    def part_of(c):
        return slice(c * span, (c + 1) * span)

    def down(hidden, c):
        return mm(hidden[0], w_down[0, :, part_of(c)]) + mm(hidden[1], w_down[1, :, part_of(c)])

    def row_of(parts, at):
        return jnp.concatenate([p[at : at + 1] for p in parts], axis=1)

    for name in ("w_gate", "w_up", "w_down"):
        loads[name].wait()
        exchange[name].wait_recv()
    pad_rows = jnp.broadcast_to(pad_gain, (TILE, main_width - width)).astype(BF16)
    pad_gate = [mm(pad_rows, w_gate[k, width:, :])[:1] for k in range(2)]
    pad_up = [mm(pad_rows, w_up[k, width:, :])[:1] for k in range(2)]

    def send_last(source):
        dest = lax.rem(source + 1, chips)
        c = remote(
            last_part.at[source],
            last_sums.at[chip],
            last_send.at[source],
            last_recv.at[chip],
            2 * dest,
        )
        return c, (core == 0) & (source < chips - 1) & (dest != chip)

    def start_last(source):
        c, needed = send_last(source)

        @pl.when(needed)
        def _():
            c.start()

    rs = []
    groups = [sends[:1], sends[1:3], *[sends[i : i + 3] for i in range(3, len(sends), 3)]]
    for group in groups:
        sources = [unflip(chip, m, chips) for m in group]
        for q in sources:
            for k in range(2):
                ref = gath.at[q, k]
                remote(ref, ref, ag_send.at[2 * q + k], ag_recv.at[2 * q + k], partner).wait_recv()
        blocks = project([gath.at[q] for q in sources])
        hidden = hidden_of(blocks)
        downs = []
        for c in range(2):
            downs.append(down(hidden, c))
            for i, q in enumerate(sources):
                part[c, q] = downs[c][i * window : (i + 1) * window].astype(BF16)
                at, to = c * chips + chip, c * chips + q
                copy = remote(
                    part.at[c, q], sums.at[c, chip], rs_send.at[to], rs_recv.at[at], same_core(q)
                )
                copy.start()
                rs.append(copy)
        for i, q in enumerate(sources):
            last_part[q] = row_of(downs, (i + 1) * window - 1)
            last_row[q] = blocks[(i + 1) * window - TILE : (i + 1) * window].astype(F32)[TILE - 1 :]
            start_last(q)

    gated[...] = (base_out[...] + carried_by(c_all) * coef_out[...]).astype(BF16)
    their_rows = pl.ds(pl.multiple_of(other * rows, rows), rows)
    my_rows = pl.ds(pl.multiple_of(core * rows, rows), rows)
    swap("gated", gated.at[their_rows], own_half.at[core])
    own_half[core] = gated[my_rows, :]
    exchange["picked"].wait_recv()
    own_rows[...] = project([gath.at[chip]])
    hidden = hidden_of(own_rows[...])
    downs = [down(hidden, c) for c in range(2)]
    for c in range(2):
        own_part[c] = downs[c][:window]
    last_part[chip] = row_of(downs, window - 1)
    start_last(chip)
    exchange["gated"].wait_recv()
    enc[...] = project([own_half])
    prev = lax.rem(chip + chips - 1, chips)
    last = last_row[prev] + last_part[prev]
    for m in masks:
        q = unflip(chip, m, chips)

        @pl.when((core == 0) & (chip > 0))
        def _(q=q):
            remote(
                last_sums.at[q], last_sums.at[q], last_send.at[q], last_recv.at[q], partner
            ).wait_recv()

        last = last + last_sums[q]
    row = lax.broadcasted_iota(jnp.int32, (window, 1), 0)
    from_before = (row == window - 1) & (core == 0) & (chip > 0)
    for c in range(2):
        result = own_rows[:, part_of(c)].astype(F32) + own_part[c]
        for m in masks:
            q = unflip(chip, m, chips)
            at, ref = c * chips + q, sums.at[c, q]
            remote(ref, ref, rs_send.at[at], rs_recv.at[at], partner).wait_recv()
            result = result + sums[c, q].astype(F32)
        table[c, core] = jnp.where(from_before, last[:, part_of(c)], result).astype(BF16)
        swap(f"table {c}", table.at[c, core], table.at[c, core])
    for c in range(2):
        exchange[f"table {c}"].wait_recv()
        expanded = mm(spread, table[c].reshape(2 * window, span))
        out[:, part_of(c)] = (enc[:, part_of(c)].astype(F32) + expanded).astype(BF16)

    for c in [*exchange.values(), *ag, *rs]:
        c.wait_send()

    @pl.when((core == 1) & (chip < chips - 1))
    def _():
        for c in halos:
            c.wait_send()

    @pl.when(chip < chips - 1)
    def _():
        for c in [*dec_copies, *st1]:
            c.wait_send()

    for h in range(SPLIT):
        for k in range(1, chips):

            @pl.when(chip != k)
            def _(h=h, k=k):
                carry(h, k).wait_send()

    for k in range(chips - 1):
        c, needed = send_last(k)

        @pl.when(needed)
        def _(c=c):
            c.wait_send()


def per_device(
    n,
    features,
    gate_in,
    conv_weight,
    conv_bias,
    log_decay,
    step_size,
    gate_gain,
    w_out,
    boundaries,
    pad_vector,
    main_gain,
    w_gate,
    w_up,
    w_down,
):
    rows, channels = features.shape
    inner = gate_in.shape[1]
    heads = log_decay.shape[1] // 2
    width = w_out.shape[1]
    bc = channels - inner
    half = inner // 2
    chips = n // 2
    piece = bc // 2 // chips
    per = boundaries.shape[0] // n
    window = 3 * per // 2
    vmem = pl.BlockSpec(memory_space=pltpu.VMEM)
    hbm = pl.BlockSpec(memory_space=pl.ANY)
    dma = pltpu.SemaphoreType.DMA
    args = (
        features,
        gate_in,
        conv_weight,
        conv_bias,
        log_decay.T,
        step_size.T,
        gate_gain,
        w_out,
        boundaries,
        pad_vector,
        main_gain,
        w_gate,
        w_up,
        w_down,
    )

    def like(a):
        return pltpu.VMEM(a.shape, a.dtype)

    def twice(a):
        return pltpu.VMEM((2, *a.shape), a.dtype)

    states = pltpu.VMEM((SPLIT * chips, piece, half // SPLIT), BF16)
    return pl.pallas_call(
        functools.partial(kernel, n, per),
        out_shape=pltpu.VMEM((rows, width), BF16),
        in_specs=[hbm] * len(args),
        out_specs=vmem,
        scratch_shapes=[
            pltpu.VMEM((2, rows, half), BF16),
            pltpu.VMEM((2, rows, bc), BF16),
            pltpu.VMEM((TILE, half), BF16),
            pltpu.VMEM((TILE, bc), BF16),
            pltpu.VMEM((2, rows, half), BF16),
            like(conv_weight),
            like(conv_bias),
            pltpu.VMEM((2, heads, rows), F32),
            pltpu.VMEM((2, heads, rows), F32),
            like(gate_gain),
            like(w_out),
            like(boundaries),
            like(pad_vector),
            like(main_gain),
            twice(w_gate),
            twice(w_up),
            twice(w_down),
            pltpu.VMEM((2, TILE + rows, half + bc), F32),
            pltpu.VMEM((2, rows, half), BF16),
            pltpu.VMEM((2, rows, bc), BF16),
            pltpu.VMEM((chips, heads, 128), F32),
            states,
            states,
            states,
            states,
            pltpu.VMEM((2 * rows, half), F32),
            pltpu.VMEM((2 * rows, half), F32),
            pltpu.VMEM((2 * rows, half), BF16),
            pltpu.VMEM((2 * window, half), F32),
            pltpu.VMEM((2 * window, half), F32),
            pltpu.VMEM((2 * window, bc // 2), BF16),
            pltpu.VMEM((window, half), BF16),
            pltpu.VMEM((2, rows, half), BF16),
            pltpu.VMEM((rows, width), BF16),
            pltpu.VMEM((chips, 2, window, half), BF16),
            pltpu.VMEM((window, width), BF16),
            pltpu.VMEM((2, chips, window, width // 2), BF16),
            pltpu.VMEM((2, window, width // 2), F32),
            pltpu.VMEM((2, chips, window, width // 2), BF16),
            pltpu.VMEM((chips, 1, width), F32),
            pltpu.VMEM((chips, 1, width), F32),
            pltpu.VMEM((chips, 1, width), F32),
            pltpu.VMEM((2, 2, window, width // 2), BF16),
            dma((16,)),
            dma((16,)),
            dma((16,)),
            dma((4,)),
            dma((2,)),
            dma((chips,)),
            dma((chips,)),
            *[dma((SPLIT * chips,)) for _ in range(4)],
            dma((n,)),
            dma((n,)),
            dma((n,)),
            dma((n,)),
            dma((chips,)),
            dma((chips,)),
            pltpu.SemaphoreType.REGULAR,
        ],
        compiler_params=pltpu.CompilerParams(collective_id=0, has_side_effects=True),
    )(*args)


def solution(mesh):
    in_specs = (
        P(("doc", "seq"), None),
        P(("doc", "seq"), None),
        P(),
        P(),
        P(("doc", "seq"), None),
        P(("doc", "seq"), None),
        P(),
        P(),
        P("doc"),
        P(),
        P(),
        P(None, "seq"),
        P(None, "seq"),
        P("seq", None),
    )
    out_specs = P(("doc", "seq"), None)
    return jax.shard_map(
        functools.partial(per_device, mesh.shape["seq"]),
        mesh=mesh,
        in_specs=in_specs,
        out_specs=out_specs,
        check_vma=False,
    )
```
